32 devices in a mesh: days: 2 (over y), sta: 8 (over z, x), win: 2 (over core).
Axes of the slice: x: 2, y: 2, z: 4, core: 2. Of those that a mesh axis runs over, the one named last changes fastest.
Arguments:
- phases: bfloat16 [48, 2048, 16], P(('days', 'win'), 'sta'), parts along dimension 0, may hold values from -3.140625 to 3.140625
- window_valid: int32 [48], P('days'), parts along dimension 0, may hold values 0 or 1
- freq_taper: float32 [2048], replicated, may hold values from 0.1 to 1.9
- pair_mask: int32 [8, 8], replicated, may hold values from 0 to 1, as said below
Outputs:
- correlations: float32 [32, 16, 512], P(('days', 'sta'), None, 'win'), parts along dimension 0
The draws below stay inside these ranges and needn't reach their ends.
There are 2 independent parts, one for each index of `days`. The reference program is written for one: setup_inputs(seed, part) draws one part's arguments, and reference() takes and returns one part's arrays. A program takes and returns all parts, laid end to end along the dimension named above; an argument that names none is the same for every part. Nothing has to cross between parts.
Inputs may be any that keep to these rules, and one draw needn't show every extreme that they name: `pair_mask`: symmetric over the two block indices; every diagonal block is kept.
All inputs are finite; a program needn't handle non-finite values.
Results may differ from the reference program's by a relative error of at most 0.005.
Values may be sent and summed in bfloat16 or wider, within the bound.
A program may use at most 64 MiB of HBM per device.

```python
import math
import jax
import jax.numpy as jnp
from jax import lax

F = 2048
LAGS = 512
WL = 12
SDEV = 2
WINDOWS = 24
STATIONS = 16
NBLK = 8
N_STA = 8
N_WIN = 2


def draw_pair_mask(key, part):
    raw_bits = jax.random.randint(key, (NBLK, NBLK), 0, 2).astype(jnp.int32)
    row_index = jnp.arange(NBLK, dtype=jnp.int32)[:, None]
    col_index = jnp.arange(NBLK, dtype=jnp.int32)[None, :]
    symmetric = jnp.where(row_index <= col_index, raw_bits, raw_bits.T)
    return jnp.where(row_index == col_index, 1, symmetric).astype(jnp.int32)


def place_ends(result, own_key, least, largest):
    spot = [jax.random.randint(jax.random.fold_in(own_key, axis), (), 0, length) for axis, length in enumerate(result.shape)]
    widest = result.shape.index(max(result.shape))
    beside = spot[:widest] + [(spot[widest] + 1) % result.shape[widest]] + spot[widest + 1:]
    return result.at[tuple(spot)].set(least).at[tuple(beside)].set(largest)


def setup_inputs(seed: int = 0, part: int = 0) -> dict:
    splits = jax.random.split(jax.random.key(seed), 5)
    part_keys = jax.random.split(jax.random.fold_in(splits[4], part), 5)
    phases = jnp.clip(jax.random.uniform(part_keys[0], (WINDOWS, F, STATIONS), jnp.float32, -3.140625, 3.140625), -3.140625, 3.140625).astype(jnp.bfloat16)
    window_valid = place_ends((jax.random.randint(part_keys[1], (WINDOWS,), 0, 4) < 3).astype(jnp.int32), jax.random.fold_in(part_keys[1], 1), 0, 1)
    freq_taper = jnp.clip(1.0 + 0.18 * jax.random.normal(splits[2], (F,), jnp.float32), 0.1, 1.9)
    pair_mask = draw_pair_mask(jax.random.fold_in(splits[4], 71), part)
    return {"phases": phases, "window_valid": window_valid, "freq_taper": freq_taper, "pair_mask": pair_mask}


def lag_table(freq_bins, lag_count):
    freq_index = jnp.arange(freq_bins, dtype=jnp.int32)[:, None]
    lag_index = jnp.arange(lag_count, dtype=jnp.int32)[None, :] - lag_count // 2
    wrapped = jnp.mod(freq_index * lag_index, 2 * freq_bins)
    angle = wrapped.astype(jnp.float32) * (math.pi / freq_bins)
    return jnp.stack((jnp.cos(angle), -jnp.sin(angle))).astype(jnp.bfloat16)

def rounded(values):
    return lax.optimization_barrier(values.astype(jnp.bfloat16)).astype(jnp.float32)

def reference(phases, window_valid, freq_taper, pair_mask):
    phase_f = phases.astype(jnp.float32)
    phasor_cos = rounded(jnp.cos(phase_f)).reshape(N_WIN, WL, F, STATIONS)
    phasor_sin = rounded(jnp.sin(phase_f)).reshape(N_WIN, WL, F, STATIONS)
    valid_f = window_valid.astype(jnp.float32)
    valid_count = jnp.sum(valid_f)
    norm_scale = 1.0 / jnp.sqrt(F * jnp.maximum(valid_count, 1.0))
    valid_groups = valid_f.reshape(N_WIN, WL)[:, :, None, None]
    weighted_cos = phasor_cos * valid_groups
    weighted_sin = phasor_sin * valid_groups
    bin_weight = freq_taper.astype(jnp.float32) * norm_scale
    lag_f = lag_table(F, LAGS).astype(jnp.float32)
    keep_full = jnp.repeat(jnp.repeat(pair_mask, SDEV, 0), SDEV, 1).astype(jnp.float32)
    keep_full = keep_full * (1.0 - jnp.eye(STATIONS, dtype=jnp.float32))
    highest = lax.Precision.HIGHEST

    def one_block(index):
        start = index * SDEV
        recv_cos = lax.dynamic_slice_in_dim(weighted_cos, start, SDEV, 3)
        recv_sin = lax.dynamic_slice_in_dim(weighted_sin, start, SDEV, 3)
        cross_re = jnp.einsum('gwki,gwkj->gijk', recv_cos, phasor_cos, precision=highest)
        cross_re = cross_re + jnp.einsum('gwki,gwkj->gijk', recv_sin, phasor_sin, precision=highest)
        cross_im = jnp.einsum('gwki,gwkj->gijk', recv_sin, phasor_cos, precision=highest)
        cross_im = cross_im - jnp.einsum('gwki,gwkj->gijk', recv_cos, phasor_sin, precision=highest)
        spec_re = lax.optimization_barrier(jnp.sum(rounded(cross_re * bin_weight), axis=0))
        spec_im = lax.optimization_barrier(jnp.sum(rounded(cross_im * bin_weight), axis=0))
        stacked = jnp.stack((spec_re, spec_im))
        correlation = jnp.einsum('cijk,ckt->ijt', stacked, lag_f, precision=highest)
        pair_keep = lax.dynamic_slice_in_dim(keep_full, start, SDEV, 0)
        return correlation * pair_keep[:, :, None]
    blocks = lax.map(one_block, jnp.arange(N_STA, dtype=jnp.int32))
    return blocks.reshape(STATIONS, STATIONS, LAGS)
```

```python
import math

import jax
import jax.numpy as jnp
import numpy as np
from jax import lax
from jax.experimental import pallas as pl
from jax.experimental.pallas import tpu as pltpu
from jax.sharding import PartitionSpec as P

LAGS = 512
MESH = pl.DeviceIdType.MESH


def fit(function, degree):
    nodes = np.polynomial.chebyshev.Chebyshev.interpolate(function, degree, domain=[0.0, math.pi**2])
    return [float(c) for c in nodes.convert(kind=np.polynomial.Polynomial).coef]


ROOT = math.sqrt(2.0)
SIN_COEF = fit(lambda y: ROOT * 0.5 * np.sinc(np.sqrt(y) / (2 * math.pi)), 4)
COS_COEF = fit(lambda y: ROOT * np.cos(0.5 * np.sqrt(y)), 4)


def horner(coef, y):
    total = y * coef[-1] + coef[-2]
    for c in coef[-3::-1]:
        total = total * y + c
    return total


def cos_sin(x):
    y = x * x
    s, c = x * horner(SIN_COEF, y), horner(COS_COEF, y)
    return 1.0 - s * s, s * c


def fused_kernel(
    phases_hbm,
    valid_hbm,
    taper_hbm,
    mask_hbm,
    out_ref,
    phases_ref,
    valid_ref,
    taper_ref,
    mask_ref,
    cos_ref,
    sin_ref,
    lag_cos,
    lag_sin,
    turn_cos,
    turn_sin,
    own,
    send,
    recv,
    load_sem,
    swap_send_sem,
    swap_recv_sem,
    send_sem,
    recv_sem,
    ready,
    *,
    sta_count,
):
    days, sta, win = (lax.axis_index(a) for a in ("days", "sta", "win"))
    win_rows, stations, band = phases_hbm.shape
    recv_rows = stations // sta_count
    freq_bins = band * sta_count
    half = LAGS // 2
    last = sta_count - 1

    loads = [
        pltpu.make_async_copy(source, target, load_sem.at[n])
        for n, (source, target) in enumerate(
            (
                (phases_hbm, phases_ref.at[win]),
                (valid_hbm, valid_ref),
                (taper_hbm, taper_ref),
                (mask_hbm, mask_ref),
            )
        )
    ]
    for load in loads:
        load.start()
    swap = pltpu.make_async_remote_copy(
        src_ref=phases_hbm,
        dst_ref=phases_ref.at[win],
        send_sem=swap_send_sem,
        recv_sem=swap_recv_sem,
        device_id=(days, sta, 1 - win),
        device_id_type=MESH,
    )

    def across(step):
        bits = [2**n for n in range(last.bit_length())]
        return sum(lax.rem(lax.div(sta, n) + lax.div(jnp.int32(step), n), 2) * n for n in bits)

    barrier = pltpu.get_barrier_semaphore()

    @pl.when(win == 1)
    def _():
        pl.semaphore_signal(barrier, inc=1, device_id=(days, sta, 0), device_id_type=MESH)

    @pl.when(win == 0)
    def _():
        pl.semaphore_wait(barrier, 1)
        pl.semaphore_signal(ready, inc=1, device_id=(days, sta, 1), device_id_type=MESH)
        swap.start()

    for step in range(last, 0, -1):
        pl.semaphore_signal(barrier, inc=1, device_id=(days, across(step), 1), device_id_type=MESH)

    rows = 16
    lag = lax.broadcasted_iota(jnp.int32, (rows, LAGS), 1) - half
    sub = lax.broadcasted_iota(jnp.int32, (rows, LAGS), 0)

    def turned(k):
        turn = ((k * lag + freq_bins) & (2 * freq_bins - 1)) - freq_bins
        return cos_sin(turn.astype(jnp.float32) * (math.pi / freq_bins))

    fine_cos, fine_sin = turned(sub)
    turn_cos[...], turn_sin[...] = turned(sub * rows + sta * band)

    @pl.when(win == 1)
    def _():
        pl.semaphore_wait(ready, 1)
        swap.start()

    for b in range(band // rows):
        c, s = turn_cos[b : b + 1, :], turn_sin[b : b + 1, :]
        at = slice(b * rows, (b + 1) * rows)
        lag_cos[at, :] = (c * fine_cos - s * fine_sin).astype(jnp.bfloat16)
        lag_sin[at, :] = (-s * fine_cos - c * fine_sin).astype(jnp.bfloat16)

    for load in loads[1:]:
        load.wait()
    count = valid_ref[0]
    for w in range(1, valid_ref.shape[0]):
        count = count + valid_ref[w]
    count = jnp.full((1, 128), count, jnp.int32).astype(jnp.float32)
    norm = 1.0 / jnp.sqrt(freq_bins * jnp.maximum(count, 1.0))
    lane_rows = band // 128
    weight = jnp.concatenate(
        [taper_ref[pl.ds(sta * lane_rows + r, 1), :] * norm for r in range(lane_rows)], axis=1
    )

    def phasors(group):
        for w in range(win_rows):
            n = group * win_rows + w
            valid = valid_ref[n].astype(jnp.float32)
            c, s = cos_sin(phases_ref[group, w].astype(jnp.float32))
            cos_ref[n] = c.astype(jnp.bfloat16).astype(jnp.float32) * valid
            sin_ref[n] = s.astype(jnp.bfloat16).astype(jnp.float32) * valid

    def cross(step):
        row = across(step) * recv_rows + win
        made = []
        for group in range(2):
            re = jnp.zeros((stations, band), jnp.float32)
            im = jnp.zeros((stations, band), jnp.float32)
            for n in range(group * win_rows, (group + 1) * win_rows):
                cj, sj = cos_ref[n], sin_ref[n]
                ci, si = cos_ref[n, pl.ds(row, 1), :], sin_ref[n, pl.ds(row, 1), :]
                re = re + (ci * cj + si * sj)
                im = im + (si * cj - ci * sj)
            made.append([(x * weight).astype(jnp.bfloat16) for x in (re, im)])
        return [jnp.concatenate(part, axis=0) for part in zip(*made)]

    def to_lags(re, im):
        part = jnp.dot(re, lag_cos[...], preferred_element_type=jnp.float32)
        part = part + jnp.dot(im, lag_sin[...], preferred_element_type=jnp.float32)
        return part[:stations] + part[stations:]

    def scatter(step, side):
        return pltpu.make_async_remote_copy(
            src_ref=send.at[2 * step + side],
            dst_ref=recv.at[2 * step + lax.rem(win + side, 2)],
            send_sem=send_sem,
            recv_sem=recv_sem,
            device_id=(days, across(step), side),
            device_id_type=MESH,
        )

    def pack(step, re, im):
        lags = to_lags(re, im).astype(jnp.bfloat16)
        for side in range(2):
            send[2 * step + side] = lags[:, side * half : (side + 1) * half]

    def push(step):
        for side in range(2):
            scatter(step, side).start()

    def step_of(n):
        step = last - n
        return jnp.where(step == sta, last, step)

    loads[0].wait()
    phasors(win)
    swap.wait_recv()
    phasors(1 - win)

    @pl.when(win == 1)
    def _():
        pl.semaphore_wait(barrier, 2 * last)
        pl.semaphore_signal(ready, inc=1, device_id=(days, sta, 0), device_id_type=MESH)

    @pl.when(win == 0)
    def _():
        pl.semaphore_wait(ready, 1)

    first = jnp.where(sta == 0, last, sta)
    pack(first, *cross(first))
    push(first)

    def chunk(n, before):
        pack(step_of(n - 1), *before)
        made = cross(step_of(n))
        push(step_of(n - 1))
        return made

    before = lax.fori_loop(2, last, chunk, cross(step_of(1)))
    pack(step_of(last - 1), *before)
    mine = cross(0)
    push(step_of(last - 1))
    lags = to_lags(*mine)
    sides = [lags[:, side * half : (side + 1) * half] for side in range(2)]
    own[...] = jnp.where(win == 0, sides[0], sides[1])
    send[0] = jnp.where(win == 0, sides[1], sides[0]).astype(jnp.bfloat16)
    back = pltpu.make_async_remote_copy(
        src_ref=send.at[0],
        dst_ref=recv.at[1],
        send_sem=send_sem,
        recv_sem=recv_sem,
        device_id=(days, sta, 1 - win),
        device_id_type=MESH,
    )
    back.start()

    source = lax.broadcasted_iota(jnp.int32, (stations, half), 0)
    keep = jnp.zeros((stations, half), jnp.float32)
    for b in range(sta_count):
        keep = jnp.where(source // recv_rows == b, mask_ref[sta, b].astype(jnp.float32), keep)

    pltpu.make_async_copy(recv.at[1:], recv.at[1:], recv_sem).wait()
    total = [own[...], recv[1].astype(jnp.float32)]
    for step in range(1, sta_count):
        for r in range(2):
            total[r] = total[r] + recv[2 * step + r].astype(jnp.float32)
    for r in range(2):
        row = lax.rem(win + r, 2)
        pair_keep = jnp.where(source == sta * recv_rows + row, 0.0, keep)
        out_ref[row] = total[r] * pair_keep
    pltpu.make_async_copy(recv.at[1:], recv.at[1:], send_sem).wait()
    swap.wait_send()


def fused(phases, window_valid, freq_taper, pair_mask):
    sta_count = lax.axis_size("sta")
    win_rows, band, stations = phases.shape
    recv_rows = stations // sta_count
    half = LAGS // 2
    f32, bf16, vmem = jnp.float32, jnp.bfloat16, pltpu.VMEM
    return pl.pallas_call(
        lambda *refs: fused_kernel(*refs, sta_count=sta_count),
        name="fused",
        out_shape=jax.ShapeDtypeStruct((recv_rows, stations, half), f32),
        in_specs=[pl.BlockSpec(memory_space=pltpu.HBM)] * 4,
        out_specs=pl.BlockSpec(memory_space=pltpu.VMEM),
        scratch_shapes=[
            vmem((2, win_rows, stations, band), bf16),
            pltpu.SMEM(window_valid.shape, jnp.int32),
            vmem((freq_taper.shape[0] // 128, 128), f32),
            pltpu.SMEM(pair_mask.shape, jnp.int32),
            vmem((2 * win_rows, stations, band), f32),
            vmem((2 * win_rows, stations, band), f32),
            vmem((band, LAGS), bf16),
            vmem((band, LAGS), bf16),
            vmem((16, LAGS), f32),
            vmem((16, LAGS), f32),
            vmem((stations, half), f32),
            vmem((2 * sta_count, stations, half), bf16),
            vmem((2 * sta_count, stations, half), bf16),
            pltpu.SemaphoreType.DMA((4,)),
            pltpu.SemaphoreType.DMA,
            pltpu.SemaphoreType.DMA,
            pltpu.SemaphoreType.DMA,
            pltpu.SemaphoreType.DMA,
            pltpu.SemaphoreType.REGULAR,
        ],
        compiler_params=pltpu.CompilerParams(
            collective_id=0, has_side_effects=True, vmem_limit_bytes=16 * 2**20
        ),
    )(
        *(
            pltpu.with_memory_space_constraint(a, pltpu.HBM)
            for a in (
                jnp.transpose(phases, (0, 2, 1)),
                window_valid,
                freq_taper.reshape(-1, 128),
                pair_mask,
            )
        )
    )


def lag_table(freq_bins, lag_count):
    freq_index = jnp.arange(freq_bins, dtype=jnp.int32)[:, None]
    lag_index = jnp.arange(lag_count, dtype=jnp.int32)[None, :] - lag_count // 2
    wrapped = jnp.mod(freq_index * lag_index, 2 * freq_bins)
    angle = wrapped.astype(jnp.float32) * (math.pi / freq_bins)
    return jnp.stack((jnp.cos(angle), -jnp.sin(angle))).astype(jnp.bfloat16)


def per_device(phases, window_valid, freq_taper, pair_mask):
    sta_count = lax.axis_size("sta")
    win_rows, band_bins, stations = phases.shape
    freq_bins = band_bins * sta_count
    recv_rows = stations // sta_count
    sta_index = lax.axis_index("sta")
    win_group = lax.axis_index("win")
    valid_count = jnp.sum(window_valid.astype(jnp.float32))
    norm_scale = 1.0 / jnp.sqrt(freq_bins * jnp.maximum(valid_count, 1.0))
    bin_weight = freq_taper * norm_scale
    group_valid = lax.dynamic_slice_in_dim(window_valid, win_group * win_rows, win_rows)
    group_weight = group_valid.astype(jnp.bfloat16)[:, None, None]
    own_f = phases.astype(jnp.float32)
    own_cos = jnp.cos(own_f).astype(jnp.bfloat16)
    own_sin = jnp.sin(own_f).astype(jnp.bfloat16)
    left_cos = own_cos * group_weight
    left_sin = own_sin * group_weight
    band_weight = lax.dynamic_slice_in_dim(bin_weight, sta_index * band_bins, band_bins)
    pair_re = jnp.einsum("wki,wkj->ijk", left_cos, own_cos, preferred_element_type=jnp.float32)
    pair_re = pair_re + jnp.einsum(
        "wki,wkj->ijk", left_sin, own_sin, preferred_element_type=jnp.float32
    )
    band_re = (pair_re * band_weight).astype(jnp.bfloat16)
    pair_im = jnp.einsum("wki,wkj->ijk", left_sin, own_cos, preferred_element_type=jnp.float32)
    pair_im = pair_im - jnp.einsum(
        "wki,wkj->ijk", left_cos, own_sin, preferred_element_type=jnp.float32
    )
    band_im = (pair_im * band_weight).astype(jnp.bfloat16)
    spectra = lax.all_to_all(
        jnp.stack((band_re, band_im)), "sta", split_axis=1, concat_axis=3, tiled=True
    )
    lag_count = LAGS
    transform = lag_table(freq_bins, lag_count)
    flat_spectra = spectra.reshape(2, recv_rows * stations, freq_bins)
    correlation = jnp.einsum(
        "cnk,ckt->nt", flat_spectra, transform, preferred_element_type=jnp.float32
    )
    block_row = lax.dynamic_index_in_dim(pair_mask, sta_index, 0, keepdims=False)
    station_row = jnp.repeat(block_row, recv_rows).astype(jnp.float32)
    receiver = sta_index * recv_rows + jnp.arange(recv_rows, dtype=jnp.int32)
    distinct = (receiver[:, None] != jnp.arange(stations, dtype=jnp.int32)[None, :]).astype(
        jnp.float32
    )
    pair_keep = station_row[None, :] * distinct
    correlation = correlation.reshape(recv_rows, stations, lag_count) * pair_keep[:, :, None]
    return lax.psum_scatter(correlation, "win", scatter_dimension=2, tiled=True)


def solution(mesh):
    def body(phases, window_valid, freq_taper, pair_mask):
        win_rows, band, stations = phases.shape
        sta_count, win_count = mesh.shape["sta"], mesh.shape["win"]
        power = band * sta_count & (band * sta_count - 1) == 0 and sta_count & (sta_count - 1) == 0
        if sta_count == 8 and band == 256 and stations == 16 and win_count == 2 and power:
            return fused(phases, window_valid, freq_taper, pair_mask)
        return per_device(phases, window_valid, freq_taper, pair_mask)

    return jax.shard_map(
        body,
        mesh=mesh,
        in_specs=(P(("days", "win"), "sta", None), P("days"), P(), P()),
        out_specs=P(("days", "sta"), None, "win"),
        check_vma=False,
    )
```

```python
import math

import jax
import jax.numpy as jnp
import numpy as np
from jax import lax
from jax.experimental import pallas as pl
from jax.experimental.pallas import tpu as pltpu
from jax.sharding import PartitionSpec as P

LAGS = 512
MESH = pl.DeviceIdType.MESH


def fit(function, degree):
    nodes = np.polynomial.chebyshev.Chebyshev.interpolate(function, degree, domain=[0.0, math.pi**2])
    return [float(c) for c in nodes.convert(kind=np.polynomial.Polynomial).coef]


ROOT = math.sqrt(2.0)
SIN_COEF = fit(lambda y: ROOT * 0.5 * np.sinc(np.sqrt(y) / (2 * math.pi)), 4)
COS_COEF = fit(lambda y: ROOT * np.cos(0.5 * np.sqrt(y)), 4)


def horner(coef, y):
    total = y * coef[-1] + coef[-2]
    for c in coef[-3::-1]:
        total = total * y + c
    return total


def cos_sin(x):
    y = x * x
    s, c = x * horner(SIN_COEF, y), horner(COS_COEF, y)
    return 1.0 - s * s, s * c


def fused_kernel(
    phases_hbm,
    valid_hbm,
    taper_hbm,
    mask_hbm,
    out_ref,
    phases_ref,
    valid_ref,
    taper_ref,
    mask_ref,
    cos_ref,
    sin_ref,
    lag_cos,
    lag_sin,
    turn_cos,
    turn_sin,
    own,
    send,
    recv,
    root_send,
    root_recv,
    load_sem,
    swap_send_sem,
    swap_recv_sem,
    send_sem,
    recv_sem,
    root_send_sem,
    root_recv_sem,
    ready,
    *,
    sta_count,
):
    days, sta, win = (lax.axis_index(a) for a in ("days", "sta", "win"))
    win_rows, stations, band = phases_hbm.shape
    recv_rows = stations // sta_count
    freq_bins = band * sta_count
    half = LAGS // 2
    last = sta_count - 1

    parts = 3
    part_rows = win_rows // parts
    copies = [(valid_hbm, valid_ref)]
    for part in range(parts):
        at = pl.ds(part * part_rows, part_rows)
        copies.append((phases_hbm.at[at], phases_ref.at[win, at]))
    copies += [(taper_hbm, taper_ref), (mask_hbm, mask_ref)]
    loads = [
        pltpu.make_async_copy(source, target, load_sem.at[n])
        for n, (source, target) in enumerate(copies)
    ]
    for load in loads:
        load.start()
    swap = pltpu.make_async_remote_copy(
        src_ref=phases_hbm,
        dst_ref=phases_ref.at[win],
        send_sem=swap_send_sem,
        recv_sem=swap_recv_sem,
        device_id=(days, sta, 1 - win),
        device_id_type=MESH,
    )

    def across(step):
        bits = [2**n for n in range(last.bit_length())]
        return sum(lax.rem(lax.div(sta, n) + lax.div(jnp.int32(step), n), 2) * n for n in bits)

    barrier = pltpu.get_barrier_semaphore()

    @pl.when(win == 1)
    def _():
        pl.semaphore_signal(barrier, inc=1, device_id=(days, sta, 0), device_id_type=MESH)

    @pl.when(sta == 0)
    def _():
        for step in range(last, 0, -1):
            pl.semaphore_signal(barrier, inc=1, device_id=(days, step, 0), device_id_type=MESH)

    @pl.when((win == 0) & (sta == 0))
    def _():
        pl.semaphore_wait(barrier, 1)

    @pl.when((win == 0) & (sta != 0))
    def _():
        pl.semaphore_wait(barrier, 3)

    @pl.when(win == 0)
    def _():
        pl.semaphore_signal(ready, inc=1, device_id=(days, sta, 1), device_id_type=MESH)
        swap.start()

    for step in range(last, 0, -1):
        pl.semaphore_signal(barrier, inc=1, device_id=(days, across(step), 1), device_id_type=MESH)

    rows = 16
    lag = lax.broadcasted_iota(jnp.int32, (rows, LAGS), 1) - half
    sub = lax.broadcasted_iota(jnp.int32, (rows, LAGS), 0)

    def turned(k):
        turn = ((k * lag + freq_bins) & (2 * freq_bins - 1)) - freq_bins
        return cos_sin(turn.astype(jnp.float32) * (math.pi / freq_bins))

    fine_cos, fine_sin = turned(sub)
    turn_cos[...], turn_sin[...] = turned(sub * rows + sta * band)

    @pl.when(win == 1)
    def _():
        pl.semaphore_wait(ready, 1)
        swap.start()

    for b in range(band // rows):
        c, s = turn_cos[b : b + 1, :], turn_sin[b : b + 1, :]
        at = slice(b * rows, (b + 1) * rows)
        lag_cos[at, :] = (c * fine_cos - s * fine_sin).astype(jnp.bfloat16)
        lag_sin[at, :] = (-s * fine_cos - c * fine_sin).astype(jnp.bfloat16)

    def phasor(group, w):
        n = group * win_rows + w
        valid = valid_ref[n].astype(jnp.float32)
        c, s = cos_sin(phases_ref[group, w].astype(jnp.float32))
        c = c.astype(jnp.bfloat16).astype(jnp.float32) * valid
        s = s.astype(jnp.bfloat16).astype(jnp.float32) * valid
        cos_ref[n], sin_ref[n] = c, s
        return c, s

    def cross(step):
        row = across(step) * recv_rows + win
        made = []
        for group in range(2):
            re = jnp.zeros((stations, band), jnp.float32)
            im = jnp.zeros((stations, band), jnp.float32)
            for n in range(group * win_rows, (group + 1) * win_rows):
                cj, sj = cos_ref[n], sin_ref[n]
                ci, si = cos_ref[n, pl.ds(row, 1), :], sin_ref[n, pl.ds(row, 1), :]
                re = re + (ci * cj + si * sj)
                im = im + (si * cj - ci * sj)
            made.append([(x * weight).astype(jnp.bfloat16) for x in (re, im)])
        return [jnp.concatenate(part, axis=0) for part in zip(*made)]

    def to_lags(re, im):
        part = jnp.dot(re, lag_cos[...], preferred_element_type=jnp.float32)
        return part + jnp.dot(im, lag_sin[...], preferred_element_type=jnp.float32)

    def scatter(step, side):
        return pltpu.make_async_remote_copy(
            src_ref=send.at[2 * step + side],
            dst_ref=recv.at[2 * step + lax.rem(win + side, 2)],
            send_sem=send_sem,
            recv_sem=recv_sem,
            device_id=(days, across(step), side),
            device_id_type=MESH,
        )

    def both(re, im):
        lags = to_lags(re, im)
        return lags[:stations] + lags[stations:]

    def pack(step, re, im):
        lags = both(re, im).astype(jnp.bfloat16)
        for side in range(2):
            send[2 * step + side] = lags[:, side * half : (side + 1) * half]

    def push(step):
        for side in range(2):
            scatter(step, side).start()

    def to_root(side, step):
        return pltpu.make_async_remote_copy(
            src_ref=root_send.at[side],
            dst_ref=root_recv.at[2 * (step - 1) + win],
            send_sem=root_send_sem,
            recv_sem=root_recv_sem,
            device_id=(days, 0, side),
            device_id_type=MESH,
        )

    re = [jnp.zeros((stations, band), jnp.float32) for _ in range(recv_rows)]
    im = [jnp.zeros((stations, band), jnp.float32) for _ in range(recv_rows)]
    loads[0].wait()
    for part in range(parts):
        loads[part + 1].wait()
        for w in range(part * part_rows, (part + 1) * part_rows):
            cj, sj = phasor(win, w)
            for r in range(recv_rows):
                ci, si = cj[r : r + 1, :], sj[r : r + 1, :]
                re[r] = re[r] + (ci * cj + si * sj)
                im[r] = im[r] + (si * cj - ci * sj)
    loads[parts + 1].wait()
    count = valid_ref[0]
    for w in range(1, valid_ref.shape[0]):
        count = count + valid_ref[w]
    count = jnp.full((1, 128), count, jnp.int32).astype(jnp.float32)
    norm = 1.0 / jnp.sqrt(freq_bins * jnp.maximum(count, 1.0))
    lane_rows = band // 128
    weight = jnp.concatenate(
        [taper_ref[pl.ds(sta * lane_rows + r, 1), :] * norm for r in range(lane_rows)], axis=1
    )

    made = [
        jnp.concatenate([(x * weight).astype(jnp.bfloat16) for x in part], axis=0)
        for part in (re, im)
    ]
    lags = to_lags(*made).astype(jnp.bfloat16)
    for side in range(2):
        root_send[side] = lags[:, side * half : (side + 1) * half]

    @pl.when(sta != 0)
    def _():
        for side in range(2):
            to_root(side, sta).start()

    swap.wait_recv()
    for w in range(win_rows):
        phasor(1 - win, w)

    def all_entered():
        @pl.when(win == 1)
        def _():
            pl.semaphore_wait(barrier, 2 * last)
            pl.semaphore_signal(ready, inc=1, device_id=(days, sta, 0), device_id_type=MESH)

        @pl.when(win == 0)
        def _():
            pl.semaphore_wait(ready, 1)

    pl.when(sta != 0)(all_entered)

    def step_of(n):
        step = last - n
        return jnp.where((step == sta) & (sta != 0), last, step)

    def chunk(n, before):
        pack(step_of(n - 1), *before)
        made = cross(step_of(n))

        @pl.when(sta != 0)
        def _():
            push(step_of(n - 1))

        return made

    least = jnp.where(sta == 0, 0, 1)
    before = lax.fori_loop(least + 1, last, chunk, cross(step_of(least)))
    pack(step_of(last - 1), *before)
    mine = cross(0)

    @pl.when(sta != 0)
    def _():
        push(step_of(last - 1))

    lags = both(*mine)
    sides = [lags[:, side * half : (side + 1) * half] for side in range(2)]
    own[...] = jnp.where(win == 0, sides[0], sides[1])
    send[0] = jnp.where(win == 0, sides[1], sides[0]).astype(jnp.bfloat16)
    back = pltpu.make_async_remote_copy(
        src_ref=send.at[0],
        dst_ref=recv.at[1],
        send_sem=send_sem,
        recv_sem=recv_sem,
        device_id=(days, sta, 1 - win),
        device_id_type=MESH,
    )
    back.start()

    loads[parts + 2].wait()
    source = lax.broadcasted_iota(jnp.int32, (stations, half), 0)
    keep = jnp.zeros((stations, half), jnp.float32)
    for b in range(sta_count):
        keep = jnp.where(source // recv_rows == b, mask_ref[sta, b].astype(jnp.float32), keep)

    def finish(total, rows):
        for r in range(2):
            pair_keep = jnp.where(source == sta * recv_rows + rows[r], 0.0, keep)
            out_ref[rows[r]] = total[r] * pair_keep

    def waits(ref, sem):
        pltpu.make_async_copy(ref, ref, sem).wait()

    @pl.when(sta != 0)
    def _():
        waits(recv.at[1:], recv_sem)
        total = [own[...], recv[1].astype(jnp.float32)]
        for step in range(1, sta_count):
            for r in range(2):
                total[r] = total[r] + recv[2 * step + r].astype(jnp.float32)
        finish(total, (win, 1 - win))
        waits(recv.at[3:], send_sem)
        waits(root_recv.at[:2], root_send_sem)

    @pl.when(sta == 0)
    def _():
        all_entered()
        for step in range(last, 0, -1):
            push(step)
        waits(recv.at[1:2], recv_sem)
        other = recv[1].astype(jnp.float32)
        total = [jnp.where(win == r, own[...], other) for r in range(2)]
        waits(root_recv, root_recv_sem)
        for m in range(2 * last):
            part = root_recv[m].astype(jnp.float32)
            for r in range(2):
                total[r] = total[r] + part[r * stations : (r + 1) * stations]
        finish(total, (0, 1))
        waits(recv.at[1:], send_sem)

    swap.wait_send()


def fused(phases, window_valid, freq_taper, pair_mask):
    sta_count = lax.axis_size("sta")
    win_rows, band, stations = phases.shape
    recv_rows = stations // sta_count
    half = LAGS // 2
    f32, bf16, vmem = jnp.float32, jnp.bfloat16, pltpu.VMEM
    return pl.pallas_call(
        lambda *refs: fused_kernel(*refs, sta_count=sta_count),
        name="fused",
        out_shape=jax.ShapeDtypeStruct((recv_rows, stations, half), f32),
        in_specs=[pl.BlockSpec(memory_space=pltpu.HBM)] * 4,
        out_specs=pl.BlockSpec(memory_space=pltpu.VMEM),
        scratch_shapes=[
            vmem((2, win_rows, stations, band), bf16),
            pltpu.SMEM(window_valid.shape, jnp.int32),
            vmem((freq_taper.shape[0] // 128, 128), f32),
            pltpu.SMEM(pair_mask.shape, jnp.int32),
            vmem((2 * win_rows, stations, band), f32),
            vmem((2 * win_rows, stations, band), f32),
            vmem((band, LAGS), bf16),
            vmem((band, LAGS), bf16),
            vmem((16, LAGS), f32),
            vmem((16, LAGS), f32),
            vmem((stations, half), f32),
            vmem((2 * sta_count, stations, half), bf16),
            vmem((2 * sta_count, stations, half), bf16),
            vmem((2, recv_rows * stations, half), bf16),
            vmem((2 * (sta_count - 1), recv_rows * stations, half), bf16),
            pltpu.SemaphoreType.DMA((6,)),
            pltpu.SemaphoreType.DMA,
            pltpu.SemaphoreType.DMA,
            pltpu.SemaphoreType.DMA,
            pltpu.SemaphoreType.DMA,
            pltpu.SemaphoreType.DMA,
            pltpu.SemaphoreType.DMA,
            pltpu.SemaphoreType.REGULAR,
        ],
        compiler_params=pltpu.CompilerParams(
            collective_id=0, has_side_effects=True, vmem_limit_bytes=16 * 2**20
        ),
    )(
        *(
            pltpu.with_memory_space_constraint(a, pltpu.HBM)
            for a in (
                jnp.transpose(phases, (0, 2, 1)),
                window_valid,
                freq_taper.reshape(-1, 128),
                pair_mask,
            )
        )
    )


def lag_table(freq_bins, lag_count):
    freq_index = jnp.arange(freq_bins, dtype=jnp.int32)[:, None]
    lag_index = jnp.arange(lag_count, dtype=jnp.int32)[None, :] - lag_count // 2
    wrapped = jnp.mod(freq_index * lag_index, 2 * freq_bins)
    angle = wrapped.astype(jnp.float32) * (math.pi / freq_bins)
    return jnp.stack((jnp.cos(angle), -jnp.sin(angle))).astype(jnp.bfloat16)


def per_device(phases, window_valid, freq_taper, pair_mask):
    sta_count = lax.axis_size("sta")
    win_rows, band_bins, stations = phases.shape
    freq_bins = band_bins * sta_count
    recv_rows = stations // sta_count
    sta_index = lax.axis_index("sta")
    win_group = lax.axis_index("win")
    valid_count = jnp.sum(window_valid.astype(jnp.float32))
    norm_scale = 1.0 / jnp.sqrt(freq_bins * jnp.maximum(valid_count, 1.0))
    bin_weight = freq_taper * norm_scale
    group_valid = lax.dynamic_slice_in_dim(window_valid, win_group * win_rows, win_rows)
    group_weight = group_valid.astype(jnp.bfloat16)[:, None, None]
    own_f = phases.astype(jnp.float32)
    own_cos = jnp.cos(own_f).astype(jnp.bfloat16)
    own_sin = jnp.sin(own_f).astype(jnp.bfloat16)
    left_cos = own_cos * group_weight
    left_sin = own_sin * group_weight
    band_weight = lax.dynamic_slice_in_dim(bin_weight, sta_index * band_bins, band_bins)
    pair_re = jnp.einsum("wki,wkj->ijk", left_cos, own_cos, preferred_element_type=jnp.float32)
    pair_re = pair_re + jnp.einsum(
        "wki,wkj->ijk", left_sin, own_sin, preferred_element_type=jnp.float32
    )
    band_re = (pair_re * band_weight).astype(jnp.bfloat16)
    pair_im = jnp.einsum("wki,wkj->ijk", left_sin, own_cos, preferred_element_type=jnp.float32)
    pair_im = pair_im - jnp.einsum(
        "wki,wkj->ijk", left_cos, own_sin, preferred_element_type=jnp.float32
    )
    band_im = (pair_im * band_weight).astype(jnp.bfloat16)
    spectra = lax.all_to_all(
        jnp.stack((band_re, band_im)), "sta", split_axis=1, concat_axis=3, tiled=True
    )
    lag_count = LAGS
    transform = lag_table(freq_bins, lag_count)
    flat_spectra = spectra.reshape(2, recv_rows * stations, freq_bins)
    correlation = jnp.einsum(
        "cnk,ckt->nt", flat_spectra, transform, preferred_element_type=jnp.float32
    )
    block_row = lax.dynamic_index_in_dim(pair_mask, sta_index, 0, keepdims=False)
    station_row = jnp.repeat(block_row, recv_rows).astype(jnp.float32)
    receiver = sta_index * recv_rows + jnp.arange(recv_rows, dtype=jnp.int32)
    distinct = (receiver[:, None] != jnp.arange(stations, dtype=jnp.int32)[None, :]).astype(
        jnp.float32
    )
    pair_keep = station_row[None, :] * distinct
    correlation = correlation.reshape(recv_rows, stations, lag_count) * pair_keep[:, :, None]
    return lax.psum_scatter(correlation, "win", scatter_dimension=2, tiled=True)


def solution(mesh):
    def body(phases, window_valid, freq_taper, pair_mask):
        win_rows, band, stations = phases.shape
        sta_count, win_count = mesh.shape["sta"], mesh.shape["win"]
        power = band * sta_count & (band * sta_count - 1) == 0 and sta_count & (sta_count - 1) == 0
        if sta_count == 8 and band == 256 and stations == 16 and win_count == 2 and power:
            return fused(phases, window_valid, freq_taper, pair_mask)
        return per_device(phases, window_valid, freq_taper, pair_mask)

    return jax.shard_map(
        body,
        mesh=mesh,
        in_specs=(P(("days", "win"), "sta", None), P("days"), P(), P()),
        out_specs=P(("days", "sta"), None, "win"),
        check_vma=False,
    )
```

```python
import math

import jax
import jax.numpy as jnp
import numpy as np
from jax import lax
from jax.experimental import pallas as pl
from jax.experimental.pallas import tpu as pltpu
from jax.sharding import PartitionSpec as P

LAGS = 512
MESH = pl.DeviceIdType.MESH


def fit(function, degree):
    nodes = np.polynomial.chebyshev.Chebyshev.interpolate(function, degree, domain=[0.0, math.pi**2])
    return [float(c) for c in nodes.convert(kind=np.polynomial.Polynomial).coef]


ROOT = math.sqrt(2.0)
SIN_COEF = fit(lambda y: ROOT * 0.5 * np.sinc(np.sqrt(y) / (2 * math.pi)), 4)
COS_COEF = fit(lambda y: ROOT * np.cos(0.5 * np.sqrt(y)), 4)


def horner(coef, y):
    total = y * coef[-1] + coef[-2]
    for c in coef[-3::-1]:
        total = total * y + c
    return total


def cos_sin(x):
    y = x * x
    s, c = x * horner(SIN_COEF, y), horner(COS_COEF, y)
    return 1.0 - s * s, s * c


def fused_kernel(
    phases_hbm,
    valid_hbm,
    taper_hbm,
    mask_hbm,
    out_ref,
    phases_ref,
    valid_ref,
    taper_ref,
    mask_ref,
    cos_ref,
    sin_ref,
    lag_cos,
    lag_sin,
    turn_cos,
    turn_sin,
    weight_ref,
    own,
    send,
    recv,
    root_send,
    root_recv,
    load_sem,
    swap_send_sem,
    swap_recv_sem,
    send_sem,
    recv_sem,
    root_send_sem,
    root_recv_sem,
    ready,
    came,
    *,
    sta_count,
):
    days, sta, win = (lax.axis_index(a) for a in ("days", "sta", "win"))
    win_rows, stations, band = phases_hbm.shape
    recv_rows = stations // sta_count
    freq_bins = band * sta_count
    half = LAGS // 2
    last = sta_count - 1

    parts = 3
    part_rows = win_rows // parts
    copies = [(valid_hbm, valid_ref)]
    for part in range(parts):
        at = pl.ds(part * part_rows, part_rows)
        copies.append((phases_hbm.at[at], phases_ref.at[win, at]))
    copies += [(taper_hbm, taper_ref), (mask_hbm, mask_ref)]
    loads = [
        pltpu.make_async_copy(source, target, load_sem.at[n])
        for n, (source, target) in enumerate(copies)
    ]
    loads[0].start()
    swaps = [
        pltpu.make_async_remote_copy(
            src_ref=phases_hbm.at[pl.ds(part * part_rows, part_rows)],
            dst_ref=phases_ref.at[win, pl.ds(part * part_rows, part_rows)],
            send_sem=swap_send_sem.at[part],
            recv_sem=swap_recv_sem.at[part],
            device_id=(days, sta, 1 - win),
            device_id_type=MESH,
        )
        for part in range(parts)
    ]

    def across(step):
        bits = [2**n for n in range(last.bit_length())]
        return sum(lax.rem(lax.div(sta, n) + lax.div(jnp.int32(step), n), 2) * n for n in bits)

    barrier = pltpu.get_barrier_semaphore()

    @pl.when(win == 1)
    def _():
        pl.semaphore_signal(barrier, inc=1, device_id=(days, sta, 0), device_id_type=MESH)

    @pl.when(sta == 0)
    def _():
        for step in range(last, 0, -1):
            pl.semaphore_signal(barrier, inc=1, device_id=(days, step, 0), device_id_type=MESH)

    @pl.when((win == 0) & (sta == 0))
    def _():
        pl.semaphore_wait(barrier, 1)

    @pl.when((win == 0) & (sta != 0))
    def _():
        pl.semaphore_wait(barrier, 3)

    @pl.when(win == 0)
    def _():
        pl.semaphore_signal(ready, inc=1, device_id=(days, sta, 1), device_id_type=MESH)
        for swap in swaps:
            swap.start()

    for load in loads[1:]:
        load.start()

    for chip in range(1, sta_count):

        @pl.when((sta != 0) & (sta != chip))
        def _():
            pl.semaphore_signal(barrier, inc=1, device_id=(days, chip, 1), device_id_type=MESH)

    rows = 16
    lag = lax.broadcasted_iota(jnp.int32, (rows, LAGS), 1) - half
    sub = lax.broadcasted_iota(jnp.int32, (rows, LAGS), 0)

    def turned(k):
        turn = ((k * lag + freq_bins) & (2 * freq_bins - 1)) - freq_bins
        return cos_sin(turn.astype(jnp.float32) * (math.pi / freq_bins))

    fine_cos, fine_sin = turned(sub)
    turn_cos[...], turn_sin[...] = turned(sub * rows + sta * band)

    @pl.when(win == 1)
    def _():
        pl.semaphore_wait(ready, 1)
        for swap in swaps:
            swap.start()

    @pl.when((win == 1) & (sta != 0))
    def _():
        for side in range(2):
            pl.semaphore_signal(
                came.at[sta], inc=1, device_id=(days, 0, side), device_id_type=MESH
            )

    for b in range(band // rows):
        c, s = turn_cos[b : b + 1, :], turn_sin[b : b + 1, :]
        at = slice(b * rows, (b + 1) * rows)
        lag_cos[at, :] = (c * fine_cos - s * fine_sin).astype(jnp.bfloat16)
        lag_sin[at, :] = (-s * fine_cos - c * fine_sin).astype(jnp.bfloat16)

    def phasor(group, w):
        n = group * win_rows + w
        valid = valid_ref[n].astype(jnp.float32)
        c, s = cos_sin(phases_ref[group, w].astype(jnp.float32))
        c = c.astype(jnp.bfloat16).astype(jnp.float32) * valid
        s = s.astype(jnp.bfloat16).astype(jnp.float32) * valid
        cos_ref[n], sin_ref[n] = c, s
        return c, s

    def cross(step):
        row = across(step) * recv_rows + win
        made = []
        for group in range(2):
            re = jnp.zeros((stations, band), jnp.float32)
            im = jnp.zeros((stations, band), jnp.float32)
            for n in range(group * win_rows, (group + 1) * win_rows):
                cj, sj = cos_ref[n], sin_ref[n]
                ci, si = cos_ref[n, pl.ds(row, 1), :], sin_ref[n, pl.ds(row, 1), :]
                re = re + (ci * cj + si * sj)
                im = im + (si * cj - ci * sj)
            made.append([(x * weight_ref[...]).astype(jnp.bfloat16) for x in (re, im)])
        return [jnp.concatenate(part, axis=0) for part in zip(*made)]

    def to_lags(re, im):
        part = jnp.dot(re, lag_cos[...], preferred_element_type=jnp.float32)
        return part + jnp.dot(im, lag_sin[...], preferred_element_type=jnp.float32)

    def scatter(step, side):
        return pltpu.make_async_remote_copy(
            src_ref=send.at[2 * step + side],
            dst_ref=recv.at[2 * step + lax.rem(win + side, 2)],
            send_sem=send_sem,
            recv_sem=recv_sem,
            device_id=(days, across(step), side),
            device_id_type=MESH,
        )

    def both(re, im):
        lags = to_lags(re, im)
        return lags[:stations] + lags[stations:]

    def pack(step, re, im):
        lags = both(re, im).astype(jnp.bfloat16)
        for side in range(2):
            send[2 * step + side] = lags[:, side * half : (side + 1) * half]

    def push(step):
        for side in range(2):
            scatter(step, side).start()

    def to_root(side, step):
        return pltpu.make_async_remote_copy(
            src_ref=root_send.at[side],
            dst_ref=root_recv.at[step - 1],
            send_sem=root_send_sem,
            recv_sem=root_recv_sem,
            device_id=(days, 0, side),
            device_id_type=MESH,
        )

    loads[0].wait()

    def arrive(group, part):
        if group == 0:
            loads[part + 1].wait()
        else:
            swaps[part].wait_recv()
        return range(part * part_rows, (part + 1) * part_rows)

    def norm_weight():
        loads[parts + 1].wait()
        count = valid_ref[0]
        for w in range(1, valid_ref.shape[0]):
            count = count + valid_ref[w]
        count = jnp.full((1, 128), count, jnp.int32).astype(jnp.float32)
        norm = 1.0 / jnp.sqrt(freq_bins * jnp.maximum(count, 1.0))
        lane_rows = band // 128
        weight_ref[...] = jnp.concatenate(
            [taper_ref[pl.ds(sta * lane_rows + r, 1), :] * norm for r in range(lane_rows)], axis=1
        )

    @pl.when(win == 0)
    def _():
        norm_weight()
        for group in range(2):
            for part in range(parts):
                for w in arrive(group, part):
                    phasor(group, w)

    @pl.when(win == 1)
    def _():
        made = []
        for group in range(2):
            re = [jnp.zeros((stations, band), jnp.float32) for _ in range(recv_rows)]
            im = [jnp.zeros((stations, band), jnp.float32) for _ in range(recv_rows)]
            for part in range(parts):
                for w in arrive(group, part):
                    cj, sj = phasor(1 - group, w)
                    for r in range(recv_rows):
                        ci, si = cj[r : r + 1, :], sj[r : r + 1, :]
                        re[r] = re[r] + (ci * cj + si * sj)
                        im[r] = im[r] + (si * cj - ci * sj)
            if group == 0:
                norm_weight()
            made.append([[(x * weight_ref[...]).astype(jnp.bfloat16) for x in p] for p in (re, im)])
        re, im = [jnp.concatenate(made[0][p] + made[1][p], axis=0) for p in range(2)]
        for side in range(2):
            at = slice(side * half, (side + 1) * half)
            lags = jnp.dot(re, lag_cos[:, at], preferred_element_type=jnp.float32)
            lags = lags + jnp.dot(im, lag_sin[:, at], preferred_element_type=jnp.float32)
            lags = lags[: recv_rows * stations] + lags[recv_rows * stations :]
            root_send[side] = lags.astype(jnp.bfloat16)

            @pl.when(sta != 0)
            def _():
                to_root(side, sta).start()

    def all_entered():
        @pl.when(win == 1)
        def _():
            pl.semaphore_wait(barrier, 2 * (last - 1))
            pl.semaphore_signal(ready, inc=1, device_id=(days, sta, 0), device_id_type=MESH)

        @pl.when(win == 0)
        def _():
            pl.semaphore_wait(ready, 1)

    late = sta != 0
    pl.when(late)(all_entered)

    def step_of(n):
        return across(n + jnp.where(n < sta, 0, 1))

    def chunk(n, before):
        pack(step_of(n - 1), *before)
        made = cross(step_of(n))

        @pl.when(late)
        def _():
            push(step_of(n - 1))

        return made

    least = jnp.where(sta == 0, 0, 1)
    before = lax.fori_loop(least + 1, last, chunk, cross(step_of(least)))
    pack(step_of(last - 1), *before)
    mine = cross(0)

    @pl.when(late)
    def _():
        push(step_of(last - 1))

    lags = both(*mine)
    sides = [lags[:, side * half : (side + 1) * half] for side in range(2)]
    own[...] = jnp.where(win == 0, sides[0], sides[1])
    send[0] = jnp.where(win == 0, sides[1], sides[0]).astype(jnp.bfloat16)
    back = pltpu.make_async_remote_copy(
        src_ref=send.at[0],
        dst_ref=recv.at[1],
        send_sem=send_sem,
        recv_sem=recv_sem,
        device_id=(days, sta, 1 - win),
        device_id_type=MESH,
    )
    back.start()

    loads[parts + 2].wait()
    source = lax.broadcasted_iota(jnp.int32, (stations, half), 0)
    keep = jnp.zeros((stations, half), jnp.float32)
    for b in range(sta_count):
        keep = jnp.where(source // recv_rows == b, mask_ref[sta, b].astype(jnp.float32), keep)

    def finish(total, rows):
        for r in range(2):
            pair_keep = jnp.where(source == sta * recv_rows + rows[r], 0.0, keep)
            out_ref[rows[r]] = total[r] * pair_keep

    def waits(ref, sem):
        pltpu.make_async_copy(ref, ref, sem).wait()

    @pl.when(sta != 0)
    def _():
        waits(recv.at[1:], recv_sem)
        total = [own[...], recv[1].astype(jnp.float32)]
        for step in range(1, sta_count):
            for r in range(2):
                total[r] = total[r] + recv[2 * step + r].astype(jnp.float32)
        finish(total, (win, 1 - win))
        waits(recv.at[3:], send_sem)

        @pl.when(win == 1)
        def _():
            waits(root_recv.at[:2], root_send_sem)

    @pl.when(sta == 0)
    def _():
        @pl.loop(1, sta_count)
        def _(step):
            pl.semaphore_wait(came.at[step], 1)
            push(step)

        waits(recv.at[1:2], recv_sem)
        other = recv[1].astype(jnp.float32)
        total = [jnp.where(win == r, own[...], other) for r in range(2)]
        waits(root_recv, root_recv_sem)
        for m in range(last):
            part = root_recv[m].astype(jnp.float32)
            for r in range(2):
                total[r] = total[r] + part[r * stations : (r + 1) * stations]
        finish(total, (0, 1))
        waits(recv.at[1:], send_sem)

    for swap in swaps:
        swap.wait_send()


def fused(phases, window_valid, freq_taper, pair_mask):
    sta_count = lax.axis_size("sta")
    win_rows, band, stations = phases.shape
    recv_rows = stations // sta_count
    half = LAGS // 2
    f32, bf16, vmem = jnp.float32, jnp.bfloat16, pltpu.VMEM
    return pl.pallas_call(
        lambda *refs: fused_kernel(*refs, sta_count=sta_count),
        name="fused",
        out_shape=jax.ShapeDtypeStruct((recv_rows, stations, half), f32),
        in_specs=[pl.BlockSpec(memory_space=pltpu.HBM)] * 4,
        out_specs=pl.BlockSpec(memory_space=pltpu.VMEM),
        scratch_shapes=[
            vmem((2, win_rows, stations, band), bf16),
            pltpu.SMEM(window_valid.shape, jnp.int32),
            vmem((freq_taper.shape[0] // 128, 128), f32),
            pltpu.SMEM(pair_mask.shape, jnp.int32),
            vmem((2 * win_rows, stations, band), f32),
            vmem((2 * win_rows, stations, band), f32),
            vmem((band, LAGS), bf16),
            vmem((band, LAGS), bf16),
            vmem((16, LAGS), f32),
            vmem((16, LAGS), f32),
            vmem((1, band), f32),
            vmem((stations, half), f32),
            vmem((2 * sta_count, stations, half), bf16),
            vmem((2 * sta_count, stations, half), bf16),
            vmem((2, recv_rows * stations, half), bf16),
            vmem((sta_count - 1, recv_rows * stations, half), bf16),
            pltpu.SemaphoreType.DMA((6,)),
            pltpu.SemaphoreType.DMA((3,)),
            pltpu.SemaphoreType.DMA((3,)),
            pltpu.SemaphoreType.DMA,
            pltpu.SemaphoreType.DMA,
            pltpu.SemaphoreType.DMA,
            pltpu.SemaphoreType.DMA,
            pltpu.SemaphoreType.REGULAR,
            pltpu.SemaphoreType.REGULAR((sta_count,)),
        ],
        compiler_params=pltpu.CompilerParams(
            collective_id=0, has_side_effects=True, vmem_limit_bytes=16 * 2**20
        ),
    )(
        *(
            pltpu.with_memory_space_constraint(a, pltpu.HBM)
            for a in (
                jnp.transpose(phases, (0, 2, 1)),
                window_valid,
                freq_taper.reshape(-1, 128),
                pair_mask,
            )
        )
    )


def lag_table(freq_bins, lag_count):
    freq_index = jnp.arange(freq_bins, dtype=jnp.int32)[:, None]
    lag_index = jnp.arange(lag_count, dtype=jnp.int32)[None, :] - lag_count // 2
    wrapped = jnp.mod(freq_index * lag_index, 2 * freq_bins)
    angle = wrapped.astype(jnp.float32) * (math.pi / freq_bins)
    return jnp.stack((jnp.cos(angle), -jnp.sin(angle))).astype(jnp.bfloat16)


def per_device(phases, window_valid, freq_taper, pair_mask):
    sta_count = lax.axis_size("sta")
    win_rows, band_bins, stations = phases.shape
    freq_bins = band_bins * sta_count
    recv_rows = stations // sta_count
    sta_index = lax.axis_index("sta")
    win_group = lax.axis_index("win")
    valid_count = jnp.sum(window_valid.astype(jnp.float32))
    norm_scale = 1.0 / jnp.sqrt(freq_bins * jnp.maximum(valid_count, 1.0))
    bin_weight = freq_taper * norm_scale
    group_valid = lax.dynamic_slice_in_dim(window_valid, win_group * win_rows, win_rows)
    group_weight = group_valid.astype(jnp.bfloat16)[:, None, None]
    own_f = phases.astype(jnp.float32)
    own_cos = jnp.cos(own_f).astype(jnp.bfloat16)
    own_sin = jnp.sin(own_f).astype(jnp.bfloat16)
    left_cos = own_cos * group_weight
    left_sin = own_sin * group_weight
    band_weight = lax.dynamic_slice_in_dim(bin_weight, sta_index * band_bins, band_bins)
    pair_re = jnp.einsum("wki,wkj->ijk", left_cos, own_cos, preferred_element_type=jnp.float32)
    pair_re = pair_re + jnp.einsum(
        "wki,wkj->ijk", left_sin, own_sin, preferred_element_type=jnp.float32
    )
    band_re = (pair_re * band_weight).astype(jnp.bfloat16)
    pair_im = jnp.einsum("wki,wkj->ijk", left_sin, own_cos, preferred_element_type=jnp.float32)
    pair_im = pair_im - jnp.einsum(
        "wki,wkj->ijk", left_cos, own_sin, preferred_element_type=jnp.float32
    )
    band_im = (pair_im * band_weight).astype(jnp.bfloat16)
    spectra = lax.all_to_all(
        jnp.stack((band_re, band_im)), "sta", split_axis=1, concat_axis=3, tiled=True
    )
    lag_count = LAGS
    transform = lag_table(freq_bins, lag_count)
    flat_spectra = spectra.reshape(2, recv_rows * stations, freq_bins)
    correlation = jnp.einsum(
        "cnk,ckt->nt", flat_spectra, transform, preferred_element_type=jnp.float32
    )
    block_row = lax.dynamic_index_in_dim(pair_mask, sta_index, 0, keepdims=False)
    station_row = jnp.repeat(block_row, recv_rows).astype(jnp.float32)
    receiver = sta_index * recv_rows + jnp.arange(recv_rows, dtype=jnp.int32)
    distinct = (receiver[:, None] != jnp.arange(stations, dtype=jnp.int32)[None, :]).astype(
        jnp.float32
    )
    pair_keep = station_row[None, :] * distinct
    correlation = correlation.reshape(recv_rows, stations, lag_count) * pair_keep[:, :, None]
    return lax.psum_scatter(correlation, "win", scatter_dimension=2, tiled=True)


def solution(mesh):
    def body(phases, window_valid, freq_taper, pair_mask):
        win_rows, band, stations = phases.shape
        sta_count, win_count = mesh.shape["sta"], mesh.shape["win"]
        power = band * sta_count & (band * sta_count - 1) == 0 and sta_count & (sta_count - 1) == 0
        if sta_count == 8 and band == 256 and stations == 16 and win_count == 2 and power:
            return fused(phases, window_valid, freq_taper, pair_mask)
        return per_device(phases, window_valid, freq_taper, pair_mask)

    return jax.shard_map(
        body,
        mesh=mesh,
        in_specs=(P(("days", "win"), "sta", None), P("days"), P(), P()),
        out_specs=P(("days", "sta"), None, "win"),
        check_vma=False,
    )
```

```python
import math

import jax
import jax.numpy as jnp
import numpy as np
from jax import lax
from jax.experimental import pallas as pl
from jax.experimental.pallas import tpu as pltpu
from jax.sharding import PartitionSpec as P

LAGS = 512
MESH = pl.DeviceIdType.MESH


def fit(function, degree):
    nodes = np.polynomial.chebyshev.Chebyshev.interpolate(function, degree, domain=[0.0, math.pi**2])
    return [float(c) for c in nodes.convert(kind=np.polynomial.Polynomial).coef]


ROOT = math.sqrt(2.0)
SIN_COEF = fit(lambda y: ROOT * 0.5 * np.sinc(np.sqrt(y) / (2 * math.pi)), 4)
COS_COEF = fit(lambda y: ROOT * np.cos(0.5 * np.sqrt(y)), 4)


def horner(coef, y):
    total = y * coef[-1] + coef[-2]
    for c in coef[-3::-1]:
        total = total * y + c
    return total


def cos_sin(x):
    y = x * x
    s, c = x * horner(SIN_COEF, y), horner(COS_COEF, y)
    return 1.0 - s * s, s * c


def fused_kernel(
    phases_hbm,
    valid_hbm,
    taper_hbm,
    mask_hbm,
    out_ref,
    phases_ref,
    valid_ref,
    taper_ref,
    mask_ref,
    cos_ref,
    sin_ref,
    lag_cos,
    lag_sin,
    turn_cos,
    turn_sin,
    weight_ref,
    own,
    send,
    recv,
    root_send,
    root_recv,
    units,
    load_sem,
    swap_sem,
    send_sem,
    recv_sem,
    ready,
    came,
    *,
    sta_count,
):
    days, sta, win = (lax.axis_index(a) for a in ("days", "sta", "win"))
    win_rows, stations, band = phases_hbm.shape
    recv_rows = stations // sta_count
    freq_bins = band * sta_count
    half = LAGS // 2
    last = sta_count - 1

    parts = swap_sem.shape[0]
    part_rows = win_rows // parts
    cut = win_rows // 2

    def unit_wait(count, sem):
        pltpu.make_async_copy(units.at[:count], units.at[:count], sem).wait()

    def phase_load(n):
        at = pl.ds(n * cut, cut)
        return pltpu.make_async_copy(phases_hbm.at[at], phases_ref.at[win, at], load_sem.at[n + 1])

    valid_load = pltpu.make_async_copy(valid_hbm, valid_ref, load_sem.at[0])
    mask_load = pltpu.make_async_copy(mask_hbm, mask_ref, load_sem.at[0])
    taper_load = pltpu.make_async_copy(taper_hbm, taper_ref, load_sem.at[2])
    valid_load.start()
    swaps = [
        pltpu.make_async_remote_copy(
            src_ref=phases_hbm.at[pl.ds(part * part_rows, part_rows)],
            dst_ref=phases_ref.at[win, pl.ds(part * part_rows, part_rows)],
            send_sem=send_sem,
            recv_sem=swap_sem.at[part],
            device_id=(days, sta, 1 - win),
            device_id_type=MESH,
        )
        for part in range(parts)
    ]

    def across(step):
        bits = [2**n for n in range(last.bit_length())]
        return sum(lax.rem(lax.div(sta, n) + lax.div(jnp.int32(step), n), 2) * n for n in bits)

    barrier = pltpu.get_barrier_semaphore()

    @pl.when(win == 1)
    def _():
        pl.semaphore_signal(barrier, inc=1, device_id=(days, sta, 0), device_id_type=MESH)

    @pl.when(sta == 0)
    def _():
        for step in range(last, 0, -1):
            pl.semaphore_signal(barrier, inc=1, device_id=(days, step, 0), device_id_type=MESH)

    @pl.when((win == 0) & (sta == 0))
    def _():
        pl.semaphore_wait(barrier, 1)

    @pl.when((win == 0) & (sta != 0))
    def _():
        pl.semaphore_wait(barrier, 3)

    @pl.when(win == 0)
    def _():
        pl.semaphore_signal(ready, inc=1, device_id=(days, sta, 1), device_id_type=MESH)
        for swap in swaps:
            swap.start()

    for load in (phase_load(0), taper_load, phase_load(1)):
        load.start()

    for chip in range(1, sta_count):

        @pl.when((sta != 0) & (sta != chip))
        def _():
            pl.semaphore_signal(barrier, inc=1, device_id=(days, chip, 1), device_id_type=MESH)

    rows = 16
    lag = lax.broadcasted_iota(jnp.int32, (rows, LAGS), 1) - half
    sub = lax.broadcasted_iota(jnp.int32, (rows, LAGS), 0)

    def turned(k):
        turn = ((k * lag + freq_bins) & (2 * freq_bins - 1)) - freq_bins
        return cos_sin(turn.astype(jnp.float32) * (math.pi / freq_bins))

    fine_cos, fine_sin = turned(sub)
    turn_cos[...], turn_sin[...] = turned(sub * rows + sta * band)

    @pl.when(win == 1)
    def _():
        pl.semaphore_wait(ready, 1)
        for swap in swaps:
            swap.start()

    @pl.when((win == 1) & (sta != 0))
    def _():
        for side in range(2):
            pl.semaphore_signal(
                came.at[lax.div(sta, last - 1)],
                inc=1,
                device_id=(days, 0, side),
                device_id_type=MESH,
            )

    for b in range(band // rows):
        c, s = turn_cos[b : b + 1, :], turn_sin[b : b + 1, :]
        at = slice(b * rows, (b + 1) * rows)
        lag_cos[at, :] = (c * fine_cos - s * fine_sin).astype(jnp.bfloat16)
        lag_sin[at, :] = (-s * fine_cos - c * fine_sin).astype(jnp.bfloat16)

    def phasor(group, w):
        n = group * win_rows + w
        valid = valid_ref[n].astype(jnp.float32)
        c, s = cos_sin(phases_ref[group, w].astype(jnp.float32))
        c = c.astype(jnp.bfloat16).astype(jnp.float32) * valid
        s = s.astype(jnp.bfloat16).astype(jnp.float32) * valid
        cos_ref[n], sin_ref[n] = c, s
        return c, s

    def cross(step):
        row = across(step) * recv_rows + win
        made = []
        for group in range(2):
            re = jnp.zeros((stations, band), jnp.float32)
            im = jnp.zeros((stations, band), jnp.float32)
            for n in range(group * win_rows, (group + 1) * win_rows):
                cj, sj = cos_ref[n], sin_ref[n]
                ci, si = cos_ref[n, pl.ds(row, 1), :], sin_ref[n, pl.ds(row, 1), :]
                re = re + (ci * cj + si * sj)
                im = im + (si * cj - ci * sj)
            made.append([(x * weight_ref[...]).astype(jnp.bfloat16) for x in (re, im)])
        return [jnp.concatenate(part, axis=0) for part in zip(*made)]

    def to_lags(re, im):
        part = jnp.dot(re, lag_cos[...], preferred_element_type=jnp.float32)
        return part + jnp.dot(im, lag_sin[...], preferred_element_type=jnp.float32)

    def scatter(step, side):
        return pltpu.make_async_remote_copy(
            src_ref=send.at[2 * step + side],
            dst_ref=recv.at[2 * step + lax.rem(win + side, 2)],
            send_sem=send_sem,
            recv_sem=recv_sem,
            device_id=(days, across(step), side),
            device_id_type=MESH,
        )

    def both(re, im):
        lags = to_lags(re, im)
        return lags[:stations] + lags[stations:]

    def pack(step, re, im):
        lags = both(re, im).astype(jnp.bfloat16)
        for side in range(2):
            send[2 * step + side] = lags[:, side * half : (side + 1) * half]

    def push(step):
        for side in range(2):
            scatter(step, side).start()

    def to_root(side, step):
        return pltpu.make_async_remote_copy(
            src_ref=root_send.at[side],
            dst_ref=root_recv.at[step - 1],
            send_sem=send_sem,
            recv_sem=recv_sem,
            device_id=(days, 0, side),
            device_id_type=MESH,
        )

    valid_load.wait()
    mask_load.start()

    def arrive(group):
        if group == 0:
            for n in range(2):
                unit_wait(cut + n, load_sem.at[n + 1])
                yield from range(n * cut, (n + 1) * cut)
        else:
            for part in range(parts):
                swaps[part].wait_recv()
                yield from range(part * part_rows, (part + 1) * part_rows)

    def norm_weight():
        count = valid_ref[0]
        for w in range(1, valid_ref.shape[0]):
            count = count + valid_ref[w]
        count = jnp.full((1, 128), count, jnp.int32).astype(jnp.float32)
        norm = 1.0 / jnp.sqrt(freq_bins * jnp.maximum(count, 1.0))
        lane_rows = band // 128
        weight_ref[...] = jnp.concatenate(
            [taper_ref[pl.ds(sta * lane_rows + r, 1), :] * norm for r in range(lane_rows)], axis=1
        )

    @pl.when(win == 0)
    def _():
        for group in range(2):
            for w in arrive(group):
                phasor(group, w)
        norm_weight()

    @pl.when(win == 1)
    def _():
        made = []
        for group in range(2):
            re = [jnp.zeros((stations, band), jnp.float32) for _ in range(recv_rows)]
            im = [jnp.zeros((stations, band), jnp.float32) for _ in range(recv_rows)]
            for w in arrive(group):
                cj, sj = phasor(1 - group, w)
                for r in range(recv_rows):
                    ci, si = cj[r : r + 1, :], sj[r : r + 1, :]
                    re[r] = re[r] + (ci * cj + si * sj)
                    im[r] = im[r] + (si * cj - ci * sj)
            if group == 0:
                norm_weight()
            made.append([[(x * weight_ref[...]).astype(jnp.bfloat16) for x in p] for p in (re, im)])
        re, im = [jnp.concatenate(made[0][p] + made[1][p], axis=0) for p in range(2)]
        for side in range(2):
            at = slice(side * half, (side + 1) * half)
            lags = jnp.dot(re, lag_cos[:, at], preferred_element_type=jnp.float32)
            lags = lags + jnp.dot(im, lag_sin[:, at], preferred_element_type=jnp.float32)
            lags = lags[: recv_rows * stations] + lags[recv_rows * stations :]
            root_send[side] = lags.astype(jnp.bfloat16)

            @pl.when(sta != 0)
            def _():
                to_root(side, sta).start()

    def all_entered():
        @pl.when(win == 1)
        def _():
            pl.semaphore_wait(barrier, 2 * (last - 1))
            pl.semaphore_signal(ready, inc=1, device_id=(days, sta, 0), device_id_type=MESH)

        @pl.when(win == 0)
        def _():
            pl.semaphore_wait(ready, 1)

    late = sta != 0
    pl.when(late)(all_entered)

    def step_of(n):
        return across(n + jnp.where(n < sta, 0, 1))

    def chunk(n, before):
        pack(step_of(n - 1), *before)
        made = cross(step_of(n))

        @pl.when(late)
        def _():
            push(step_of(n - 1))

        return made

    least = jnp.where(sta == 0, 0, 1)
    before = lax.fori_loop(least + 1, last, chunk, cross(step_of(least)))
    pack(step_of(last - 1), *before)
    mine = cross(0)

    @pl.when(late)
    def _():
        push(step_of(last - 1))

    lags = both(*mine)
    sides = [lags[:, side * half : (side + 1) * half] for side in range(2)]
    own[...] = jnp.where(win == 0, sides[0], sides[1])
    send[0] = jnp.where(win == 0, sides[1], sides[0]).astype(jnp.bfloat16)
    back = pltpu.make_async_remote_copy(
        src_ref=send.at[0],
        dst_ref=recv.at[1],
        send_sem=send_sem,
        recv_sem=recv_sem,
        device_id=(days, sta, 1 - win),
        device_id_type=MESH,
    )
    back.start()

    mask_load.wait()
    source = lax.broadcasted_iota(jnp.int32, (stations, half), 0)
    keep = jnp.zeros((stations, half), jnp.float32)
    for b in range(sta_count):
        keep = jnp.where(source // recv_rows == b, mask_ref[sta, b].astype(jnp.float32), keep)

    def finish(total, rows):
        for r in range(2):
            pair_keep = jnp.where(source == sta * recv_rows + rows[r], 0.0, keep)
            out_ref[rows[r]] = total[r] * pair_keep

    @pl.when(sta == 0)
    def _():
        for which, chips in enumerate((range(1, last - 1), range(last - 1, sta_count))):
            pl.semaphore_wait(came.at[which], len(chips))
            for chip in chips:
                push(chip)

    unit_wait(2 * sta_count - 1, recv_sem)

    @pl.when(sta != 0)
    def _():
        total = [own[...], recv[1].astype(jnp.float32)]
        for step in range(1, sta_count):
            for r in range(2):
                total[r] = total[r] + recv[2 * step + r].astype(jnp.float32)
        finish(total, (win, 1 - win))

    @pl.when(sta == 0)
    def _():
        other = recv[1].astype(jnp.float32)
        total = [jnp.where(win == r, own[...], other) for r in range(2)]
        for m in range(last):
            part = root_recv[m].astype(jnp.float32)
            for r in range(2):
                total[r] = total[r] + part[r * stations : (r + 1) * stations]
        finish(total, (0, 1))

    sent = win_rows + 2 * last - 1

    @pl.when(sta == 0)
    def _():
        unit_wait(sent + 2, send_sem)

    @pl.when((sta != 0) & (win == 0))
    def _():
        unit_wait(sent, send_sem)

    @pl.when((sta != 0) & (win == 1))
    def _():
        unit_wait(sent + 2 * recv_rows, send_sem)


def fused(phases, window_valid, freq_taper, pair_mask):
    sta_count = lax.axis_size("sta")
    win_rows, band, stations = phases.shape
    recv_rows = stations // sta_count
    half = LAGS // 2
    f32, bf16, vmem = jnp.float32, jnp.bfloat16, pltpu.VMEM
    return pl.pallas_call(
        lambda *refs: fused_kernel(*refs, sta_count=sta_count),
        name="fused",
        out_shape=jax.ShapeDtypeStruct((recv_rows, stations, half), f32),
        in_specs=[pl.BlockSpec(memory_space=pltpu.HBM)] * 4,
        out_specs=pl.BlockSpec(memory_space=pltpu.VMEM),
        scratch_shapes=[
            vmem((2, win_rows, stations, band), bf16),
            pltpu.SMEM(window_valid.shape, jnp.int32),
            vmem((freq_taper.shape[0] // 128, 128), f32),
            pltpu.SMEM(pair_mask.shape, jnp.int32),
            vmem((2 * win_rows, stations, band), f32),
            vmem((2 * win_rows, stations, band), f32),
            vmem((band, LAGS), bf16),
            vmem((band, LAGS), bf16),
            vmem((16, LAGS), f32),
            vmem((16, LAGS), f32),
            vmem((1, band), f32),
            vmem((stations, half), f32),
            vmem((2 * sta_count, stations, half), bf16),
            vmem((2 * sta_count, stations, half), bf16),
            vmem((2, recv_rows * stations, half), bf16),
            vmem((sta_count - 1, recv_rows * stations, half), bf16),
            vmem((32, stations, half), bf16),
            pltpu.SemaphoreType.DMA((3,)),
            pltpu.SemaphoreType.DMA((3,)),
            pltpu.SemaphoreType.DMA,
            pltpu.SemaphoreType.DMA,
            pltpu.SemaphoreType.REGULAR,
            pltpu.SemaphoreType.REGULAR((2,)),
        ],
        compiler_params=pltpu.CompilerParams(
            collective_id=0, has_side_effects=True, vmem_limit_bytes=16 * 2**20
        ),
    )(
        *(
            pltpu.with_memory_space_constraint(a, pltpu.HBM)
            for a in (
                jnp.transpose(phases, (0, 2, 1)),
                window_valid,
                freq_taper.reshape(-1, 128),
                pair_mask,
            )
        )
    )


def lag_table(freq_bins, lag_count):
    freq_index = jnp.arange(freq_bins, dtype=jnp.int32)[:, None]
    lag_index = jnp.arange(lag_count, dtype=jnp.int32)[None, :] - lag_count // 2
    wrapped = jnp.mod(freq_index * lag_index, 2 * freq_bins)
    angle = wrapped.astype(jnp.float32) * (math.pi / freq_bins)
    return jnp.stack((jnp.cos(angle), -jnp.sin(angle))).astype(jnp.bfloat16)


def per_device(phases, window_valid, freq_taper, pair_mask):
    sta_count = lax.axis_size("sta")
    win_rows, band_bins, stations = phases.shape
    freq_bins = band_bins * sta_count
    recv_rows = stations // sta_count
    sta_index = lax.axis_index("sta")
    win_group = lax.axis_index("win")
    valid_count = jnp.sum(window_valid.astype(jnp.float32))
    norm_scale = 1.0 / jnp.sqrt(freq_bins * jnp.maximum(valid_count, 1.0))
    bin_weight = freq_taper * norm_scale
    group_valid = lax.dynamic_slice_in_dim(window_valid, win_group * win_rows, win_rows)
    group_weight = group_valid.astype(jnp.bfloat16)[:, None, None]
    own_f = phases.astype(jnp.float32)
    own_cos = jnp.cos(own_f).astype(jnp.bfloat16)
    own_sin = jnp.sin(own_f).astype(jnp.bfloat16)
    left_cos = own_cos * group_weight
    left_sin = own_sin * group_weight
    band_weight = lax.dynamic_slice_in_dim(bin_weight, sta_index * band_bins, band_bins)
    pair_re = jnp.einsum("wki,wkj->ijk", left_cos, own_cos, preferred_element_type=jnp.float32)
    pair_re = pair_re + jnp.einsum(
        "wki,wkj->ijk", left_sin, own_sin, preferred_element_type=jnp.float32
    )
    band_re = (pair_re * band_weight).astype(jnp.bfloat16)
    pair_im = jnp.einsum("wki,wkj->ijk", left_sin, own_cos, preferred_element_type=jnp.float32)
    pair_im = pair_im - jnp.einsum(
        "wki,wkj->ijk", left_cos, own_sin, preferred_element_type=jnp.float32
    )
    band_im = (pair_im * band_weight).astype(jnp.bfloat16)
    spectra = lax.all_to_all(
        jnp.stack((band_re, band_im)), "sta", split_axis=1, concat_axis=3, tiled=True
    )
    lag_count = LAGS
    transform = lag_table(freq_bins, lag_count)
    flat_spectra = spectra.reshape(2, recv_rows * stations, freq_bins)
    correlation = jnp.einsum(
        "cnk,ckt->nt", flat_spectra, transform, preferred_element_type=jnp.float32
    )
    block_row = lax.dynamic_index_in_dim(pair_mask, sta_index, 0, keepdims=False)
    station_row = jnp.repeat(block_row, recv_rows).astype(jnp.float32)
    receiver = sta_index * recv_rows + jnp.arange(recv_rows, dtype=jnp.int32)
    distinct = (receiver[:, None] != jnp.arange(stations, dtype=jnp.int32)[None, :]).astype(
        jnp.float32
    )
    pair_keep = station_row[None, :] * distinct
    correlation = correlation.reshape(recv_rows, stations, lag_count) * pair_keep[:, :, None]
    return lax.psum_scatter(correlation, "win", scatter_dimension=2, tiled=True)


def solution(mesh):
    def body(phases, window_valid, freq_taper, pair_mask):
        win_rows, band, stations = phases.shape
        sta_count, win_count = mesh.shape["sta"], mesh.shape["win"]
        if sta_count == 8 and band == 256 and stations == 16 and win_count == 2 and win_rows == 12:
            return fused(phases, window_valid, freq_taper, pair_mask)
        return per_device(phases, window_valid, freq_taper, pair_mask)

    return jax.shard_map(
        body,
        mesh=mesh,
        in_specs=(P(("days", "win"), "sta", None), P("days"), P(), P()),
        out_specs=P(("days", "sta"), None, "win"),
        check_vma=False,
    )
```

```python
import math

import jax
import jax.numpy as jnp
import numpy as np
from jax import lax
from jax.experimental import pallas as pl
from jax.experimental.pallas import tpu as pltpu
from jax.sharding import PartitionSpec as P

LAGS = 512
MESH = pl.DeviceIdType.MESH


def fit(function, degree):
    nodes = np.polynomial.chebyshev.Chebyshev.interpolate(function, degree, domain=[0.0, math.pi**2])
    return [float(c) for c in nodes.convert(kind=np.polynomial.Polynomial).coef]


ROOT = math.sqrt(2.0)
SIN_COEF = fit(lambda y: ROOT * 0.5 * np.sinc(np.sqrt(y) / (2 * math.pi)), 4)
COS_COEF = fit(lambda y: ROOT * np.cos(0.5 * np.sqrt(y)), 4)


def horner(coef, y):
    total = y * coef[-1] + coef[-2]
    for c in coef[-3::-1]:
        total = total * y + c
    return total


def cos_sin(x, one=1.0):
    y = x * x
    s, c = x * horner(SIN_COEF, y), horner(COS_COEF, y)
    return one - s * s, s * c


def fused_kernel(
    phases_hbm,
    valid_hbm,
    taper_hbm,
    mask_hbm,
    out_ref,
    phases_ref,
    valid_ref,
    taper_ref,
    mask_ref,
    cos_ref,
    sin_ref,
    lag_cos,
    lag_sin,
    turn_cos,
    turn_sin,
    weight_ref,
    own,
    send,
    recv,
    root_send,
    root_recv,
    units,
    load_sem,
    swap_sem,
    send_sem,
    recv_sem,
    ready,
    came,
    *,
    sta_count,
):
    days, sta, win = (lax.axis_index(a) for a in ("days", "sta", "win"))
    win_rows, stations, band = phases_hbm.shape
    recv_rows = stations // sta_count
    freq_bins = band * sta_count
    half = LAGS // 2
    last = sta_count - 1

    parts = swap_sem.shape[0]
    part_rows = win_rows // parts
    cut = win_rows // 3

    def unit_wait(count, sem):
        pltpu.make_async_copy(units.at[:count], units.at[:count], sem).wait()

    def phase_load(n):
        at = pl.ds(n * cut, cut + n * cut)
        return pltpu.make_async_copy(phases_hbm.at[at], phases_ref.at[win, at], load_sem.at[n + 1])

    valid_load = pltpu.make_async_copy(valid_hbm, valid_ref, load_sem.at[0])
    mask_load = pltpu.make_async_copy(mask_hbm, mask_ref, load_sem.at[0])
    taper_load = pltpu.make_async_copy(taper_hbm, taper_ref, load_sem.at[2])
    valid_load.start()
    swaps = [
        pltpu.make_async_remote_copy(
            src_ref=phases_hbm.at[pl.ds(part * part_rows, part_rows)],
            dst_ref=phases_ref.at[win, pl.ds(part * part_rows, part_rows)],
            send_sem=send_sem,
            recv_sem=swap_sem.at[part],
            device_id=(days, sta, 1 - win),
            device_id_type=MESH,
        )
        for part in range(parts)
    ]

    def across(step):
        bits = [2**n for n in range(last.bit_length())]
        return sum(lax.rem(lax.div(sta, n) + lax.div(jnp.int32(step), n), 2) * n for n in bits)

    barrier = pltpu.get_barrier_semaphore()

    @pl.when(win == 1)
    def _():
        pl.semaphore_signal(barrier, inc=1, device_id=(days, sta, 0), device_id_type=MESH)

    @pl.when(sta == 0)
    def _():
        for step in range(last, 0, -1):
            pl.semaphore_signal(barrier, inc=1, device_id=(days, step, 0), device_id_type=MESH)

    @pl.when((win == 0) & (sta == 0))
    def _():
        pl.semaphore_wait(barrier, 1)

    @pl.when((win == 0) & (sta != 0))
    def _():
        pl.semaphore_wait(barrier, 3)

    @pl.when(win == 0)
    def _():
        pl.semaphore_signal(ready, inc=1, device_id=(days, sta, 1), device_id_type=MESH)
        for swap in swaps:
            swap.start()

    for load in (phase_load(0), taper_load, phase_load(1)):
        load.start()

    for chip in range(1, sta_count):

        @pl.when((sta != 0) & (sta != chip))
        def _():
            pl.semaphore_signal(barrier, inc=1, device_id=(days, chip, 1), device_id_type=MESH)

    rows = 16
    lag = lax.broadcasted_iota(jnp.int32, (rows, LAGS), 1) - half
    sub = lax.broadcasted_iota(jnp.int32, (rows, LAGS), 0)

    def turned(k):
        turn = ((k * lag + freq_bins) & (2 * freq_bins - 1)) - freq_bins
        return cos_sin(turn.astype(jnp.float32) * (math.pi / freq_bins))

    fine_cos, fine_sin = turned(sub)
    turn_cos[...], turn_sin[...] = turned(sub * rows + sta * band)

    @pl.when(win == 1)
    def _():
        pl.semaphore_wait(ready, 1)
        for swap in swaps:
            swap.start()

    @pl.when((win == 1) & (sta != 0))
    def _():
        for side in range(2):
            pl.semaphore_signal(
                came.at[lax.div(sta, last - 1)],
                inc=1,
                device_id=(days, 0, side),
                device_id_type=MESH,
            )

    for b in range(band // rows):
        c, s = turn_cos[b : b + 1, :], turn_sin[b : b + 1, :]
        at = slice(b * rows, (b + 1) * rows)
        lag_cos[at, :] = (c * fine_cos - s * fine_sin).astype(jnp.bfloat16)
        lag_sin[at, :] = (-s * fine_cos - c * fine_sin).astype(jnp.bfloat16)

    def phasor(group, w):
        n = group * win_rows + w
        valid = valid_ref[n].astype(jnp.float32)
        c, s = cos_sin(phases_ref[group, w].astype(jnp.float32) * valid, valid)
        c = c.astype(jnp.bfloat16).astype(jnp.float32)
        s = s.astype(jnp.bfloat16).astype(jnp.float32)
        cos_ref[n], sin_ref[n] = c, s
        return c, s

    def cross(step):
        row = across(step) * recv_rows + win
        made = []
        for group in range(2):
            re = jnp.zeros((stations, band), jnp.float32)
            im = jnp.zeros((stations, band), jnp.float32)
            for n in range(group * win_rows, (group + 1) * win_rows):
                cj, sj = cos_ref[n], sin_ref[n]
                ci, si = cos_ref[n, pl.ds(row, 1), :], sin_ref[n, pl.ds(row, 1), :]
                re = re + (ci * cj + si * sj)
                im = im + (si * cj - ci * sj)
            made.append([(x * weight_ref[...]).astype(jnp.bfloat16) for x in (re, im)])
        return [jnp.concatenate(part, axis=0) for part in zip(*made)]

    def to_lags(re, im):
        part = jnp.dot(re, lag_cos[...], preferred_element_type=jnp.float32)
        return part + jnp.dot(im, lag_sin[...], preferred_element_type=jnp.float32)

    def scatter(step, side):
        return pltpu.make_async_remote_copy(
            src_ref=send.at[2 * step + side],
            dst_ref=recv.at[2 * step + lax.rem(win + side, 2)],
            send_sem=send_sem,
            recv_sem=recv_sem,
            device_id=(days, across(step), side),
            device_id_type=MESH,
        )

    def both(re, im):
        lags = to_lags(re, im)
        return lags[:stations] + lags[stations:]

    def pack(step, re, im):
        lags = both(re, im).astype(jnp.bfloat16)
        for side in range(2):
            send[2 * step + side] = lags[:, side * half : (side + 1) * half]

    def push(step):
        for side in range(2):
            scatter(step, side).start()

    def to_root(side, step):
        return pltpu.make_async_remote_copy(
            src_ref=root_send.at[side],
            dst_ref=root_recv.at[step - 1],
            send_sem=send_sem,
            recv_sem=recv_sem,
            device_id=(days, 0, side),
            device_id_type=MESH,
        )

    valid_load.wait()
    mask_load.start()

    def arrive(group):
        if group == 0:
            for n in range(2):
                rows = cut + n * cut
                unit_wait(rows + n, load_sem.at[n + 1])
                yield from range(n * cut, n * cut + rows)
        else:
            for part in range(parts):
                swaps[part].wait_recv()
                yield from range(part * part_rows, (part + 1) * part_rows)

    def norm_weight():
        count = valid_ref[0]
        for w in range(1, valid_ref.shape[0]):
            count = count + valid_ref[w]
        count = jnp.full((1, 128), count, jnp.int32).astype(jnp.float32)
        norm = 1.0 / jnp.sqrt(freq_bins * jnp.maximum(count, 1.0))
        lane_rows = band // 128
        weight_ref[...] = jnp.concatenate(
            [taper_ref[pl.ds(sta * lane_rows + r, 1), :] * norm for r in range(lane_rows)], axis=1
        )

    @pl.when(win == 0)
    def _():
        for group in range(2):
            for w in arrive(group):
                phasor(group, w)
        norm_weight()

    @pl.when(win == 1)
    def _():
        made = []
        for group in range(2):
            re = [jnp.zeros((stations, band), jnp.float32) for _ in range(recv_rows)]
            im = [jnp.zeros((stations, band), jnp.float32) for _ in range(recv_rows)]
            for w in arrive(group):
                cj, sj = phasor(1 - group, w)
                for r in range(recv_rows):
                    ci, si = cj[r : r + 1, :], sj[r : r + 1, :]
                    re[r] = re[r] + (ci * cj + si * sj)
                    im[r] = im[r] + (si * cj - ci * sj)
            if group == 0:
                norm_weight()
            made.append([[(x * weight_ref[...]).astype(jnp.bfloat16) for x in p] for p in (re, im)])
        re, im = [jnp.concatenate(made[0][p] + made[1][p], axis=0) for p in range(2)]
        for side in range(2):
            at = slice(side * half, (side + 1) * half)
            lags = jnp.dot(re, lag_cos[:, at], preferred_element_type=jnp.float32)
            lags = lags + jnp.dot(im, lag_sin[:, at], preferred_element_type=jnp.float32)
            lags = lags[: recv_rows * stations] + lags[recv_rows * stations :]
            root_send[side] = lags.astype(jnp.bfloat16)

            @pl.when(sta != 0)
            def _():
                to_root(side, sta).start()

    def all_entered():
        @pl.when(win == 1)
        def _():
            pl.semaphore_wait(barrier, 2 * (last - 1))
            pl.semaphore_signal(ready, inc=1, device_id=(days, sta, 0), device_id_type=MESH)

        @pl.when(win == 0)
        def _():
            pl.semaphore_wait(ready, 1)

    late = sta != 0
    pl.when(late)(all_entered)

    def step_of(n):
        plain = n + jnp.where(n < sta, 0, 1)
        place = n + jnp.where(n < jnp.where(sta == 3, 5, 3 - sta), 0, 1)
        ranked = jnp.int32(0)
        for p, d in enumerate((2, 1, 4, 6, 3, 5, 7)):
            ranked = jnp.where(place == p + 1, d, ranked)
        return across(jnp.where((sta > 0) & (sta < 4), ranked, plain))

    def chunk(n, before):
        pack(step_of(n - 1), *before)
        made = cross(step_of(n))

        @pl.when(late)
        def _():
            push(step_of(n - 1))

        return made

    least = jnp.where(sta == 0, 0, 1)
    before = lax.fori_loop(least + 1, last, chunk, cross(step_of(least)))
    pack(step_of(last - 1), *before)
    mine = cross(0)

    @pl.when(late)
    def _():
        push(step_of(last - 1))

    lags = both(*mine)
    sides = [lags[:, side * half : (side + 1) * half] for side in range(2)]
    own[...] = jnp.where(win == 0, sides[0], sides[1])
    send[0] = jnp.where(win == 0, sides[1], sides[0]).astype(jnp.bfloat16)
    back = pltpu.make_async_remote_copy(
        src_ref=send.at[0],
        dst_ref=recv.at[1],
        send_sem=send_sem,
        recv_sem=recv_sem,
        device_id=(days, sta, 1 - win),
        device_id_type=MESH,
    )
    back.start()

    mask_load.wait()
    source = lax.broadcasted_iota(jnp.int32, (stations, half), 0)
    keep = jnp.zeros((stations, half), jnp.float32)
    for b in range(sta_count):
        keep = jnp.where(source // recv_rows == b, mask_ref[sta, b].astype(jnp.float32), keep)

    def finish(total, rows):
        for r in range(2):
            pair_keep = jnp.where(source == sta * recv_rows + rows[r], 0.0, keep)
            out_ref[rows[r]] = total[r] * pair_keep

    @pl.when(sta == 0)
    def _():
        for which, chips in enumerate((range(1, last - 1), range(last - 1, sta_count))):
            pl.semaphore_wait(came.at[which], len(chips))
            for chip in chips:
                push(chip)

    unit_wait(2 * sta_count - 1, recv_sem)

    @pl.when(sta != 0)
    def _():
        total = [own[...], recv[1].astype(jnp.float32)]
        for step in range(1, sta_count):
            for r in range(2):
                total[r] = total[r] + recv[2 * step + r].astype(jnp.float32)
        finish(total, (win, 1 - win))

    @pl.when(sta == 0)
    def _():
        other = recv[1].astype(jnp.float32)
        total = [jnp.where(win == r, own[...], other) for r in range(2)]
        for m in range(last):
            part = root_recv[m].astype(jnp.float32)
            for r in range(2):
                total[r] = total[r] + part[r * stations : (r + 1) * stations]
        finish(total, (0, 1))

    sent = win_rows + 2 * last - 1

    @pl.when(sta == 0)
    def _():
        unit_wait(sent + 2, send_sem)

    @pl.when((sta != 0) & (win == 0))
    def _():
        unit_wait(sent, send_sem)

    @pl.when((sta != 0) & (win == 1))
    def _():
        unit_wait(sent + 2 * recv_rows, send_sem)


def fused(phases, window_valid, freq_taper, pair_mask):
    sta_count = lax.axis_size("sta")
    win_rows, band, stations = phases.shape
    recv_rows = stations // sta_count
    half = LAGS // 2
    f32, bf16, vmem = jnp.float32, jnp.bfloat16, pltpu.VMEM
    return pl.pallas_call(
        lambda *refs: fused_kernel(*refs, sta_count=sta_count),
        name="fused",
        out_shape=jax.ShapeDtypeStruct((recv_rows, stations, half), f32),
        in_specs=[pl.BlockSpec(memory_space=pltpu.HBM)] * 4,
        out_specs=pl.BlockSpec(memory_space=pltpu.VMEM),
        scratch_shapes=[
            vmem((2, win_rows, stations, band), bf16),
            pltpu.SMEM(window_valid.shape, jnp.int32),
            vmem((freq_taper.shape[0] // 128, 128), f32),
            pltpu.SMEM(pair_mask.shape, jnp.int32),
            vmem((2 * win_rows, stations, band), f32),
            vmem((2 * win_rows, stations, band), f32),
            vmem((band, LAGS), bf16),
            vmem((band, LAGS), bf16),
            vmem((16, LAGS), f32),
            vmem((16, LAGS), f32),
            vmem((1, band), f32),
            vmem((stations, half), f32),
            vmem((2 * sta_count, stations, half), bf16),
            vmem((2 * sta_count, stations, half), bf16),
            vmem((2, recv_rows * stations, half), bf16),
            vmem((sta_count - 1, recv_rows * stations, half), bf16),
            vmem((32, stations, half), bf16),
            pltpu.SemaphoreType.DMA((3,)),
            pltpu.SemaphoreType.DMA((3,)),
            pltpu.SemaphoreType.DMA,
            pltpu.SemaphoreType.DMA,
            pltpu.SemaphoreType.REGULAR,
            pltpu.SemaphoreType.REGULAR((2,)),
        ],
        compiler_params=pltpu.CompilerParams(
            collective_id=0, has_side_effects=True, vmem_limit_bytes=16 * 2**20
        ),
    )(
        *(
            pltpu.with_memory_space_constraint(a, pltpu.HBM)
            for a in (
                jnp.transpose(phases, (0, 2, 1)),
                window_valid,
                freq_taper.reshape(-1, 128),
                pair_mask,
            )
        )
    )


def lag_table(freq_bins, lag_count):
    freq_index = jnp.arange(freq_bins, dtype=jnp.int32)[:, None]
    lag_index = jnp.arange(lag_count, dtype=jnp.int32)[None, :] - lag_count // 2
    wrapped = jnp.mod(freq_index * lag_index, 2 * freq_bins)
    angle = wrapped.astype(jnp.float32) * (math.pi / freq_bins)
    return jnp.stack((jnp.cos(angle), -jnp.sin(angle))).astype(jnp.bfloat16)


def per_device(phases, window_valid, freq_taper, pair_mask):
    sta_count = lax.axis_size("sta")
    win_rows, band_bins, stations = phases.shape
    freq_bins = band_bins * sta_count
    recv_rows = stations // sta_count
    sta_index = lax.axis_index("sta")
    win_group = lax.axis_index("win")
    valid_count = jnp.sum(window_valid.astype(jnp.float32))
    norm_scale = 1.0 / jnp.sqrt(freq_bins * jnp.maximum(valid_count, 1.0))
    bin_weight = freq_taper * norm_scale
    group_valid = lax.dynamic_slice_in_dim(window_valid, win_group * win_rows, win_rows)
    group_weight = group_valid.astype(jnp.bfloat16)[:, None, None]
    own_f = phases.astype(jnp.float32)
    own_cos = jnp.cos(own_f).astype(jnp.bfloat16)
    own_sin = jnp.sin(own_f).astype(jnp.bfloat16)
    left_cos = own_cos * group_weight
    left_sin = own_sin * group_weight
    band_weight = lax.dynamic_slice_in_dim(bin_weight, sta_index * band_bins, band_bins)
    pair_re = jnp.einsum("wki,wkj->ijk", left_cos, own_cos, preferred_element_type=jnp.float32)
    pair_re = pair_re + jnp.einsum(
        "wki,wkj->ijk", left_sin, own_sin, preferred_element_type=jnp.float32
    )
    band_re = (pair_re * band_weight).astype(jnp.bfloat16)
    pair_im = jnp.einsum("wki,wkj->ijk", left_sin, own_cos, preferred_element_type=jnp.float32)
    pair_im = pair_im - jnp.einsum(
        "wki,wkj->ijk", left_cos, own_sin, preferred_element_type=jnp.float32
    )
    band_im = (pair_im * band_weight).astype(jnp.bfloat16)
    spectra = lax.all_to_all(
        jnp.stack((band_re, band_im)), "sta", split_axis=1, concat_axis=3, tiled=True
    )
    lag_count = LAGS
    transform = lag_table(freq_bins, lag_count)
    flat_spectra = spectra.reshape(2, recv_rows * stations, freq_bins)
    correlation = jnp.einsum(
        "cnk,ckt->nt", flat_spectra, transform, preferred_element_type=jnp.float32
    )
    block_row = lax.dynamic_index_in_dim(pair_mask, sta_index, 0, keepdims=False)
    station_row = jnp.repeat(block_row, recv_rows).astype(jnp.float32)
    receiver = sta_index * recv_rows + jnp.arange(recv_rows, dtype=jnp.int32)
    distinct = (receiver[:, None] != jnp.arange(stations, dtype=jnp.int32)[None, :]).astype(
        jnp.float32
    )
    pair_keep = station_row[None, :] * distinct
    correlation = correlation.reshape(recv_rows, stations, lag_count) * pair_keep[:, :, None]
    return lax.psum_scatter(correlation, "win", scatter_dimension=2, tiled=True)


def solution(mesh):
    def body(phases, window_valid, freq_taper, pair_mask):
        win_rows, band, stations = phases.shape
        sta_count, win_count = mesh.shape["sta"], mesh.shape["win"]
        if sta_count == 8 and band == 256 and stations == 16 and win_count == 2 and win_rows == 12:
            return fused(phases, window_valid, freq_taper, pair_mask)
        return per_device(phases, window_valid, freq_taper, pair_mask)

    return jax.shard_map(
        body,
        mesh=mesh,
        in_specs=(P(("days", "win"), "sta", None), P("days"), P(), P()),
        out_specs=P(("days", "sta"), None, "win"),
        check_vma=False,
    )
```

```python
import math

import jax
import jax.numpy as jnp
import numpy as np
from jax import lax
from jax.experimental import pallas as pl
from jax.experimental.pallas import tpu as pltpu
from jax.sharding import PartitionSpec as P

LAGS = 512
MESH = pl.DeviceIdType.MESH


def fit(function, degree):
    nodes = np.polynomial.chebyshev.Chebyshev.interpolate(function, degree, domain=[0.0, math.pi**2])
    return [float(c) for c in nodes.convert(kind=np.polynomial.Polynomial).coef]


ROOT = math.sqrt(2.0)
SIN_COEF = fit(lambda y: ROOT * 0.5 * np.sinc(np.sqrt(y) / (2 * math.pi)), 4)
COS_COEF = fit(lambda y: ROOT * np.cos(0.5 * np.sqrt(y)), 4)


def horner(coef, y):
    total = y * coef[-1] + coef[-2]
    for c in coef[-3::-1]:
        total = total * y + c
    return total


def cos_sin(x, one=1.0):
    y = x * x
    s, c = x * horner(SIN_COEF, y), horner(COS_COEF, y)
    return one - s * s, s * c


def fused_kernel(
    phases_hbm,
    valid_hbm,
    taper_hbm,
    mask_hbm,
    out_ref,
    phases_ref,
    valid_ref,
    taper_ref,
    mask_ref,
    cos_ref,
    sin_ref,
    lag_cos,
    lag_sin,
    turn_cos,
    turn_sin,
    weight_ref,
    own,
    send,
    recv,
    root_send,
    root_recv,
    units,
    load_sem,
    swap_sem,
    send_sem,
    recv_sem,
    ready,
    came,
    *,
    sta_count,
):
    days, sta, win = (lax.axis_index(a) for a in ("days", "sta", "win"))
    win_rows, stations, band = phases_hbm.shape
    recv_rows = stations // sta_count
    freq_bins = band * sta_count
    half = LAGS // 2
    last = sta_count - 1

    pieces = ((0, win_rows // 3), (win_rows // 3, win_rows))

    def unit_wait(count, sem):
        pltpu.make_async_copy(units.at[:count], units.at[:count], sem).wait()

    def phase_load(n):
        at = pl.ds(pieces[n][0], pieces[n][1] - pieces[n][0])
        return pltpu.make_async_copy(phases_hbm.at[at], phases_ref.at[win, at], load_sem.at[n + 1])

    valid_load = pltpu.make_async_copy(valid_hbm, valid_ref, load_sem.at[0])
    mask_load = pltpu.make_async_copy(mask_hbm, mask_ref, load_sem.at[0])
    taper_load = pltpu.make_async_copy(taper_hbm, taper_ref, load_sem.at[2])
    valid_load.start()
    swaps = [
        pltpu.make_async_remote_copy(
            src_ref=phases_hbm.at[pl.ds(least, most - least)],
            dst_ref=phases_ref.at[win, pl.ds(least, most - least)],
            send_sem=send_sem,
            recv_sem=swap_sem.at[part],
            device_id=(days, sta, 1 - win),
            device_id_type=MESH,
        )
        for part, (least, most) in enumerate(pieces)
    ]

    def across(step):
        bits = [2**n for n in range(last.bit_length())]
        return sum(lax.rem(lax.div(sta, n) + lax.div(jnp.int32(step), n), 2) * n for n in bits)

    barrier = pltpu.get_barrier_semaphore()

    @pl.when(win == 1)
    def _():
        pl.semaphore_signal(barrier, inc=1, device_id=(days, sta, 0), device_id_type=MESH)

    @pl.when(sta == 0)
    def _():
        for step in range(last, 0, -1):
            pl.semaphore_signal(barrier, inc=1, device_id=(days, step, 0), device_id_type=MESH)

    @pl.when((win == 0) & (sta == 0))
    def _():
        pl.semaphore_wait(barrier, 1)

    @pl.when((win == 0) & (sta != 0))
    def _():
        pl.semaphore_wait(barrier, 3)

    @pl.when(win == 0)
    def _():
        pl.semaphore_signal(ready, inc=1, device_id=(days, sta, 1), device_id_type=MESH)
        for swap in swaps:
            swap.start()

    for load in (phase_load(0), taper_load, phase_load(1)):
        load.start()

    for chip in range(1, sta_count):

        @pl.when((sta != 0) & (sta != chip))
        def _():
            pl.semaphore_signal(barrier, inc=1, device_id=(days, chip, 1), device_id_type=MESH)

    rows = 16
    lag = lax.broadcasted_iota(jnp.int32, (rows, LAGS), 1) - half
    sub = lax.broadcasted_iota(jnp.int32, (rows, LAGS), 0)

    def turned(k):
        turn = ((k * lag + freq_bins) & (2 * freq_bins - 1)) - freq_bins
        return cos_sin(turn.astype(jnp.float32) * (math.pi / freq_bins))

    fine_cos, fine_sin = turned(sub)
    turn_cos[...], turn_sin[...] = turned(sub * rows + sta * band)

    @pl.when(win == 1)
    def _():
        pl.semaphore_wait(ready, 1)
        for swap in swaps:
            swap.start()

    @pl.when((win == 1) & (sta != 0))
    def _():
        for side in range(2):
            pl.semaphore_signal(
                came.at[lax.div(sta, last - 1)],
                inc=1,
                device_id=(days, 0, side),
                device_id_type=MESH,
            )

    for b in range(band // rows):
        c, s = turn_cos[b : b + 1, :], turn_sin[b : b + 1, :]
        at = slice(b * rows, (b + 1) * rows)
        lag_cos[at, :] = (c * fine_cos - s * fine_sin).astype(jnp.bfloat16)
        lag_sin[at, :] = (-s * fine_cos - c * fine_sin).astype(jnp.bfloat16)

    def phasor(group, w):
        n = group * win_rows + w
        valid = valid_ref[n].astype(jnp.float32)
        c, s = cos_sin(phases_ref[group, w].astype(jnp.float32) * valid, valid)
        c = c.astype(jnp.bfloat16).astype(jnp.float32)
        s = s.astype(jnp.bfloat16).astype(jnp.float32)
        cos_ref[n], sin_ref[n] = c, s
        return c, s

    def cross(step):
        row = across(step) * recv_rows + win
        made = []
        for group in range(2):
            re = jnp.zeros((stations, band), jnp.float32)
            im = jnp.zeros((stations, band), jnp.float32)
            for n in range(group * win_rows, (group + 1) * win_rows):
                cj, sj = cos_ref[n], sin_ref[n]
                ci, si = cos_ref[n, pl.ds(row, 1), :], sin_ref[n, pl.ds(row, 1), :]
                re = re + (ci * cj + si * sj)
                im = im + (si * cj - ci * sj)
            made.append([(x * weight_ref[...]).astype(jnp.bfloat16) for x in (re, im)])
        return [jnp.concatenate(part, axis=0) for part in zip(*made)]

    def to_lags(re, im):
        part = jnp.dot(re, lag_cos[...], preferred_element_type=jnp.float32)
        return part + jnp.dot(im, lag_sin[...], preferred_element_type=jnp.float32)

    def scatter(step, side):
        return pltpu.make_async_remote_copy(
            src_ref=send.at[2 * step + side],
            dst_ref=recv.at[2 * step + lax.rem(win + side, 2)],
            send_sem=send_sem,
            recv_sem=recv_sem,
            device_id=(days, across(step), side),
            device_id_type=MESH,
        )

    def both(re, im):
        lags = to_lags(re, im)
        return lags[:stations] + lags[stations:]

    def pack(step, re, im):
        lags = both(re, im).astype(jnp.bfloat16)
        for side in range(2):
            send[2 * step + side] = lags[:, side * half : (side + 1) * half]

    def push(step):
        for side in range(2):
            scatter(step, side).start()

    def to_root(side, step):
        return pltpu.make_async_remote_copy(
            src_ref=root_send.at[side],
            dst_ref=root_recv.at[step - 1],
            send_sem=send_sem,
            recv_sem=recv_sem,
            device_id=(days, 0, side),
            device_id_type=MESH,
        )

    valid_load.wait()
    mask_load.start()

    def arrive(group):
        for n, (least, most) in enumerate(pieces):
            if group == 0:
                unit_wait(most - least + n, load_sem.at[n + 1])
            else:
                swaps[n].wait_recv()
            yield from range(least, most)

    def norm_weight():
        count = valid_ref[0]
        for w in range(1, valid_ref.shape[0]):
            count = count + valid_ref[w]
        count = jnp.full((1, 128), count, jnp.int32).astype(jnp.float32)
        norm = 1.0 / jnp.sqrt(freq_bins * jnp.maximum(count, 1.0))
        lane_rows = band // 128
        weight_ref[...] = jnp.concatenate(
            [taper_ref[pl.ds(sta * lane_rows + r, 1), :] * norm for r in range(lane_rows)], axis=1
        )

    @pl.when(win == 0)
    def _():
        for group in range(2):
            for w in arrive(group):
                phasor(group, w)
        norm_weight()

    @pl.when(win == 1)
    def _():
        made = []
        for group in range(2):
            re = [jnp.zeros((stations, band), jnp.float32) for _ in range(recv_rows)]
            im = [jnp.zeros((stations, band), jnp.float32) for _ in range(recv_rows)]
            for w in arrive(group):
                cj, sj = phasor(1 - group, w)
                for r in range(recv_rows):
                    ci, si = cj[r : r + 1, :], sj[r : r + 1, :]
                    re[r] = re[r] + (ci * cj + si * sj)
                    im[r] = im[r] + (si * cj - ci * sj)
            if group == 0:
                norm_weight()
            made.append([[(x * weight_ref[...]).astype(jnp.bfloat16) for x in p] for p in (re, im)])
        re, im = [jnp.concatenate(made[0][p] + made[1][p], axis=0) for p in range(2)]
        for side in range(2):
            at = slice(side * half, (side + 1) * half)
            lags = jnp.dot(re, lag_cos[:, at], preferred_element_type=jnp.float32)
            lags = lags + jnp.dot(im, lag_sin[:, at], preferred_element_type=jnp.float32)
            lags = lags[: recv_rows * stations] + lags[recv_rows * stations :]
            root_send[side] = lags.astype(jnp.bfloat16)

            @pl.when(sta != 0)
            def _():
                to_root(side, sta).start()

    def all_entered():
        @pl.when(win == 1)
        def _():
            pl.semaphore_wait(barrier, 2 * (last - 1))
            pl.semaphore_signal(ready, inc=1, device_id=(days, sta, 0), device_id_type=MESH)

        @pl.when(win == 0)
        def _():
            pl.semaphore_wait(ready, 1)

    late = sta != 0
    pl.when(late)(all_entered)

    def step_of(n):
        plain = n + jnp.where(n < sta, 0, 1)
        place = n + jnp.where(n < jnp.where(sta == 3, 5, 3 - sta), 0, 1)
        ranked = jnp.int32(0)
        for p, d in enumerate((2, 1, 4, 6, 3, 5, 7)):
            ranked = jnp.where(place == p + 1, d, ranked)
        return across(jnp.where((sta > 0) & (sta < 4), ranked, plain))

    def chunk(n, before):
        pack(step_of(n - 1), *before)
        made = cross(step_of(n))

        @pl.when(late)
        def _():
            push(step_of(n - 1))

        return made

    least = jnp.where(sta == 0, 0, 1)
    before = lax.fori_loop(least + 1, last, chunk, cross(step_of(least)))
    pack(step_of(last - 1), *before)
    mine = cross(0)

    @pl.when(late)
    def _():
        push(step_of(last - 1))

    lags = both(*mine)
    sides = [lags[:, side * half : (side + 1) * half] for side in range(2)]
    own[...] = jnp.where(win == 0, sides[0], sides[1])
    send[0] = jnp.where(win == 0, sides[1], sides[0]).astype(jnp.bfloat16)
    back = pltpu.make_async_remote_copy(
        src_ref=send.at[0],
        dst_ref=recv.at[1],
        send_sem=send_sem,
        recv_sem=recv_sem,
        device_id=(days, sta, 1 - win),
        device_id_type=MESH,
    )
    back.start()

    mask_load.wait()
    source = lax.broadcasted_iota(jnp.int32, (stations, half), 0)
    keep = jnp.zeros((stations, half), jnp.float32)
    for b in range(sta_count):
        keep = jnp.where(source // recv_rows == b, mask_ref[sta, b].astype(jnp.float32), keep)

    def finish(total, rows):
        for r in range(2):
            pair_keep = jnp.where(source == sta * recv_rows + rows[r], 0.0, keep)
            out_ref[rows[r]] = total[r] * pair_keep

    @pl.when(sta == 0)
    def _():
        for which, chips in enumerate((range(1, last - 1), range(last - 1, sta_count))):
            pl.semaphore_wait(came.at[which], len(chips))
            for chip in chips:
                push(chip)

    unit_wait(2 * sta_count - 1, recv_sem)

    @pl.when(sta != 0)
    def _():
        total = [own[...], recv[1].astype(jnp.float32)]
        for step in range(1, sta_count):
            for r in range(2):
                total[r] = total[r] + recv[2 * step + r].astype(jnp.float32)
        finish(total, (win, 1 - win))

    @pl.when(sta == 0)
    def _():
        other = recv[1].astype(jnp.float32)
        total = [jnp.where(win == r, own[...], other) for r in range(2)]
        for m in range(last):
            part = root_recv[m].astype(jnp.float32)
            for r in range(2):
                total[r] = total[r] + part[r * stations : (r + 1) * stations]
        finish(total, (0, 1))

    sent = win_rows + 2 * last - 1

    @pl.when(sta == 0)
    def _():
        unit_wait(sent + 2, send_sem)

    @pl.when((sta != 0) & (win == 0))
    def _():
        unit_wait(sent, send_sem)

    @pl.when((sta != 0) & (win == 1))
    def _():
        unit_wait(sent + 2 * recv_rows, send_sem)


def fused(phases, window_valid, freq_taper, pair_mask):
    sta_count = lax.axis_size("sta")
    win_rows, band, stations = phases.shape
    recv_rows = stations // sta_count
    half = LAGS // 2
    f32, bf16, vmem = jnp.float32, jnp.bfloat16, pltpu.VMEM
    return pl.pallas_call(
        lambda *refs: fused_kernel(*refs, sta_count=sta_count),
        name="fused",
        out_shape=jax.ShapeDtypeStruct((recv_rows, stations, half), f32),
        in_specs=[pl.BlockSpec(memory_space=pltpu.HBM)] * 4,
        out_specs=pl.BlockSpec(memory_space=pltpu.VMEM),
        scratch_shapes=[
            vmem((2, win_rows, stations, band), bf16),
            pltpu.SMEM(window_valid.shape, jnp.int32),
            vmem((freq_taper.shape[0] // 128, 128), f32),
            pltpu.SMEM(pair_mask.shape, jnp.int32),
            vmem((2 * win_rows, stations, band), f32),
            vmem((2 * win_rows, stations, band), f32),
            vmem((band, LAGS), bf16),
            vmem((band, LAGS), bf16),
            vmem((16, LAGS), f32),
            vmem((16, LAGS), f32),
            vmem((1, band), f32),
            vmem((stations, half), f32),
            vmem((2 * sta_count, stations, half), bf16),
            vmem((2 * sta_count, stations, half), bf16),
            vmem((2, recv_rows * stations, half), bf16),
            vmem((sta_count - 1, recv_rows * stations, half), bf16),
            vmem((32, stations, half), bf16),
            pltpu.SemaphoreType.DMA((3,)),
            pltpu.SemaphoreType.DMA((2,)),
            pltpu.SemaphoreType.DMA,
            pltpu.SemaphoreType.DMA,
            pltpu.SemaphoreType.REGULAR,
            pltpu.SemaphoreType.REGULAR((2,)),
        ],
        compiler_params=pltpu.CompilerParams(
            collective_id=0, has_side_effects=True, vmem_limit_bytes=16 * 2**20
        ),
    )(
        *(
            pltpu.with_memory_space_constraint(a, pltpu.HBM)
            for a in (
                jnp.transpose(phases, (0, 2, 1)),
                window_valid,
                freq_taper.reshape(-1, 128),
                pair_mask,
            )
        )
    )


def lag_table(freq_bins, lag_count):
    freq_index = jnp.arange(freq_bins, dtype=jnp.int32)[:, None]
    lag_index = jnp.arange(lag_count, dtype=jnp.int32)[None, :] - lag_count // 2
    wrapped = jnp.mod(freq_index * lag_index, 2 * freq_bins)
    angle = wrapped.astype(jnp.float32) * (math.pi / freq_bins)
    return jnp.stack((jnp.cos(angle), -jnp.sin(angle))).astype(jnp.bfloat16)


def per_device(phases, window_valid, freq_taper, pair_mask):
    sta_count = lax.axis_size("sta")
    win_rows, band_bins, stations = phases.shape
    freq_bins = band_bins * sta_count
    recv_rows = stations // sta_count
    sta_index = lax.axis_index("sta")
    win_group = lax.axis_index("win")
    valid_count = jnp.sum(window_valid.astype(jnp.float32))
    norm_scale = 1.0 / jnp.sqrt(freq_bins * jnp.maximum(valid_count, 1.0))
    bin_weight = freq_taper * norm_scale
    group_valid = lax.dynamic_slice_in_dim(window_valid, win_group * win_rows, win_rows)
    group_weight = group_valid.astype(jnp.bfloat16)[:, None, None]
    own_f = phases.astype(jnp.float32)
    own_cos = jnp.cos(own_f).astype(jnp.bfloat16)
    own_sin = jnp.sin(own_f).astype(jnp.bfloat16)
    left_cos = own_cos * group_weight
    left_sin = own_sin * group_weight
    band_weight = lax.dynamic_slice_in_dim(bin_weight, sta_index * band_bins, band_bins)
    pair_re = jnp.einsum("wki,wkj->ijk", left_cos, own_cos, preferred_element_type=jnp.float32)
    pair_re = pair_re + jnp.einsum(
        "wki,wkj->ijk", left_sin, own_sin, preferred_element_type=jnp.float32
    )
    band_re = (pair_re * band_weight).astype(jnp.bfloat16)
    pair_im = jnp.einsum("wki,wkj->ijk", left_sin, own_cos, preferred_element_type=jnp.float32)
    pair_im = pair_im - jnp.einsum(
        "wki,wkj->ijk", left_cos, own_sin, preferred_element_type=jnp.float32
    )
    band_im = (pair_im * band_weight).astype(jnp.bfloat16)
    spectra = lax.all_to_all(
        jnp.stack((band_re, band_im)), "sta", split_axis=1, concat_axis=3, tiled=True
    )
    lag_count = LAGS
    transform = lag_table(freq_bins, lag_count)
    flat_spectra = spectra.reshape(2, recv_rows * stations, freq_bins)
    correlation = jnp.einsum(
        "cnk,ckt->nt", flat_spectra, transform, preferred_element_type=jnp.float32
    )
    block_row = lax.dynamic_index_in_dim(pair_mask, sta_index, 0, keepdims=False)
    station_row = jnp.repeat(block_row, recv_rows).astype(jnp.float32)
    receiver = sta_index * recv_rows + jnp.arange(recv_rows, dtype=jnp.int32)
    distinct = (receiver[:, None] != jnp.arange(stations, dtype=jnp.int32)[None, :]).astype(
        jnp.float32
    )
    pair_keep = station_row[None, :] * distinct
    correlation = correlation.reshape(recv_rows, stations, lag_count) * pair_keep[:, :, None]
    return lax.psum_scatter(correlation, "win", scatter_dimension=2, tiled=True)


def solution(mesh):
    def body(phases, window_valid, freq_taper, pair_mask):
        win_rows, band, stations = phases.shape
        sta_count, win_count = mesh.shape["sta"], mesh.shape["win"]
        if sta_count == 8 and band == 256 and stations == 16 and win_count == 2 and win_rows == 12:
            return fused(phases, window_valid, freq_taper, pair_mask)
        return per_device(phases, window_valid, freq_taper, pair_mask)

    return jax.shard_map(
        body,
        mesh=mesh,
        in_specs=(P(("days", "win"), "sta", None), P("days"), P(), P()),
        out_specs=P(("days", "sta"), None, "win"),
        check_vma=False,
    )
```

```python
import math

import jax
import jax.numpy as jnp
import numpy as np
from jax import lax
from jax.experimental import pallas as pl
from jax.experimental.pallas import tpu as pltpu
from jax.sharding import PartitionSpec as P

LAGS = 512
MESH = pl.DeviceIdType.MESH


def fit(function, degree):
    nodes = np.polynomial.chebyshev.Chebyshev.interpolate(function, degree, domain=[0.0, math.pi**2])
    return [float(c) for c in nodes.convert(kind=np.polynomial.Polynomial).coef]


ROOT = math.sqrt(2.0)
SIN_COEF = fit(lambda y: ROOT * 0.5 * np.sinc(np.sqrt(y) / (2 * math.pi)), 4)
COS_COEF = fit(lambda y: ROOT * np.cos(0.5 * np.sqrt(y)), 4)


def horner(coef, y):
    total = y * coef[-1] + coef[-2]
    for c in coef[-3::-1]:
        total = total * y + c
    return total


def cos_sin(x, one=1.0):
    y = x * x
    s, c = x * horner(SIN_COEF, y), horner(COS_COEF, y)
    return one - s * s, s * c


def fused_kernel(
    phases_hbm,
    valid_hbm,
    taper_hbm,
    mask_hbm,
    out_ref,
    phases_ref,
    valid_ref,
    taper_ref,
    mask_ref,
    cos_ref,
    sin_ref,
    lag_cos,
    lag_sin,
    turn_cos,
    turn_sin,
    weight_ref,
    own,
    send,
    recv,
    root_send,
    root_recv,
    units,
    load_sem,
    swap_sem,
    send_sem,
    recv_sem,
    ready,
    came,
    *,
    sta_count,
):
    days, sta, win = (lax.axis_index(a) for a in ("days", "sta", "win"))
    win_rows, stations, band = phases_hbm.shape
    recv_rows = stations // sta_count
    freq_bins = band * sta_count
    half = LAGS // 2
    last = sta_count - 1

    pieces = ((0, win_rows // 2), (win_rows // 2, win_rows))

    def unit_wait(count, sem):
        pltpu.make_async_copy(units.at[:count], units.at[:count], sem).wait()

    def phase_load(n):
        at = pl.ds(pieces[n][0], pieces[n][1] - pieces[n][0])
        return pltpu.make_async_copy(phases_hbm.at[at], phases_ref.at[win, at], load_sem.at[n + 1])

    valid_load = pltpu.make_async_copy(valid_hbm, valid_ref, load_sem.at[0])
    mask_load = pltpu.make_async_copy(mask_hbm, mask_ref, load_sem.at[0])
    taper_load = pltpu.make_async_copy(taper_hbm, taper_ref, load_sem.at[2])
    valid_load.start()
    swaps = [
        pltpu.make_async_remote_copy(
            src_ref=phases_hbm.at[pl.ds(least, most - least)],
            dst_ref=phases_ref.at[win, pl.ds(least, most - least)],
            send_sem=send_sem,
            recv_sem=swap_sem.at[part],
            device_id=(days, sta, 1 - win),
            device_id_type=MESH,
        )
        for part, (least, most) in enumerate(pieces)
    ]

    def across(step):
        bits = [2**n for n in range(last.bit_length())]
        return sum(lax.rem(lax.div(sta, n) + lax.div(jnp.int32(step), n), 2) * n for n in bits)

    barrier = pltpu.get_barrier_semaphore()

    @pl.when(win == 1)
    def _():
        pl.semaphore_signal(barrier, inc=1, device_id=(days, sta, 0), device_id_type=MESH)

    @pl.when(sta == 0)
    def _():
        for step in range(last, 0, -1):
            pl.semaphore_signal(barrier, inc=1, device_id=(days, step, 0), device_id_type=MESH)

    @pl.when((win == 0) & (sta == 0))
    def _():
        pl.semaphore_wait(barrier, 1)

    @pl.when((win == 0) & (sta != 0))
    def _():
        pl.semaphore_wait(barrier, 3)

    @pl.when(win == 0)
    def _():
        pl.semaphore_signal(ready, inc=1, device_id=(days, sta, 1), device_id_type=MESH)
        for swap in swaps:
            swap.start()

    for load in (phase_load(0), taper_load, phase_load(1)):
        load.start()

    for chip in range(1, sta_count):

        @pl.when((sta != 0) & (sta != chip))
        def _():
            pl.semaphore_signal(barrier, inc=1, device_id=(days, chip, 1), device_id_type=MESH)

    rows = 16
    lag = lax.broadcasted_iota(jnp.int32, (rows, LAGS), 1) - half
    sub = lax.broadcasted_iota(jnp.int32, (rows, LAGS), 0)

    def turned(k):
        turn = ((k * lag + freq_bins) & (2 * freq_bins - 1)) - freq_bins
        return cos_sin(turn.astype(jnp.float32) * (math.pi / freq_bins))

    fine_cos, fine_sin = turned(sub)
    turn_cos[...], turn_sin[...] = turned(sub * rows + sta * band)

    @pl.when(win == 1)
    def _():
        pl.semaphore_wait(ready, 1)
        for swap in swaps:
            swap.start()

    @pl.when((win == 1) & (sta != 0))
    def _():
        for side in range(2):
            pl.semaphore_signal(
                came.at[lax.div(sta, last - 1)],
                inc=1,
                device_id=(days, 0, side),
                device_id_type=MESH,
            )

    for b in range(band // rows):
        c, s = turn_cos[b : b + 1, :], turn_sin[b : b + 1, :]
        at = slice(b * rows, (b + 1) * rows)
        lag_cos[at, :] = (c * fine_cos - s * fine_sin).astype(jnp.bfloat16)
        lag_sin[at, :] = (-s * fine_cos - c * fine_sin).astype(jnp.bfloat16)

    def phasor(group, w):
        n = group * win_rows + w
        valid = valid_ref[n].astype(jnp.float32)
        c, s = cos_sin(phases_ref[group, w].astype(jnp.float32) * valid, valid)
        c = c.astype(jnp.bfloat16).astype(jnp.float32)
        s = s.astype(jnp.bfloat16).astype(jnp.float32)
        cos_ref[n], sin_ref[n] = c, s
        return c, s

    def cross(step):
        row = across(step) * recv_rows + win
        made = []
        for group in range(2):
            re = jnp.zeros((stations, band), jnp.float32)
            im = jnp.zeros((stations, band), jnp.float32)
            for n in range(group * win_rows, (group + 1) * win_rows):
                cj, sj = cos_ref[n], sin_ref[n]
                ci, si = cos_ref[n, pl.ds(row, 1), :], sin_ref[n, pl.ds(row, 1), :]
                re = re + (ci * cj + si * sj)
                im = im + (si * cj - ci * sj)
            made.append([(x * weight_ref[...]).astype(jnp.bfloat16) for x in (re, im)])
        return [jnp.concatenate(part, axis=0) for part in zip(*made)]

    def to_lags(re, im):
        part = jnp.dot(re, lag_cos[...], preferred_element_type=jnp.float32)
        return part + jnp.dot(im, lag_sin[...], preferred_element_type=jnp.float32)

    def scatter(step, side):
        return pltpu.make_async_remote_copy(
            src_ref=send.at[2 * step + side],
            dst_ref=recv.at[2 * step + lax.rem(win + side, 2)],
            send_sem=send_sem,
            recv_sem=recv_sem,
            device_id=(days, across(step), side),
            device_id_type=MESH,
        )

    def both(re, im):
        lags = to_lags(re, im)
        return lags[:stations] + lags[stations:]

    def pack(step, re, im):
        lags = both(re, im).astype(jnp.bfloat16)
        for side in range(2):
            send[2 * step + side] = lags[:, side * half : (side + 1) * half]

    def push(step):
        for side in range(2):
            scatter(step, side).start()

    def to_root(side, step):
        return pltpu.make_async_remote_copy(
            src_ref=root_send.at[side],
            dst_ref=root_recv.at[step - 1],
            send_sem=send_sem,
            recv_sem=recv_sem,
            device_id=(days, 0, side),
            device_id_type=MESH,
        )

    valid_load.wait()
    mask_load.start()

    def arrive(group):
        for n, (least, most) in enumerate(pieces):
            if group == 0:
                unit_wait(most - least + n, load_sem.at[n + 1])
            else:
                swaps[n].wait_recv()
            yield from range(least, most)

    def norm_weight():
        count = valid_ref[0]
        for w in range(1, valid_ref.shape[0]):
            count = count + valid_ref[w]
        count = jnp.full((1, 128), count, jnp.int32).astype(jnp.float32)
        norm = 1.0 / jnp.sqrt(freq_bins * jnp.maximum(count, 1.0))
        lane_rows = band // 128
        weight_ref[...] = jnp.concatenate(
            [taper_ref[pl.ds(sta * lane_rows + r, 1), :] * norm for r in range(lane_rows)], axis=1
        )

    @pl.when(win == 0)
    def _():
        for group in range(2):
            for w in arrive(group):
                phasor(group, w)
        norm_weight()

    @pl.when(win == 1)
    def _():
        made = []
        for group in range(2):
            re = [jnp.zeros((stations, band), jnp.float32) for _ in range(recv_rows)]
            im = [jnp.zeros((stations, band), jnp.float32) for _ in range(recv_rows)]
            for w in arrive(group):
                cj, sj = phasor(1 - group, w)
                for r in range(recv_rows):
                    ci, si = cj[r : r + 1, :], sj[r : r + 1, :]
                    re[r] = re[r] + (ci * cj + si * sj)
                    im[r] = im[r] + (si * cj - ci * sj)
            if group == 0:
                norm_weight()
            made.append([[(x * weight_ref[...]).astype(jnp.bfloat16) for x in p] for p in (re, im)])
        re, im = [jnp.concatenate(made[0][p] + made[1][p], axis=0) for p in range(2)]
        for side in range(2):
            at = slice(side * half, (side + 1) * half)
            lags = jnp.dot(re, lag_cos[:, at], preferred_element_type=jnp.float32)
            lags = lags + jnp.dot(im, lag_sin[:, at], preferred_element_type=jnp.float32)
            lags = lags[: recv_rows * stations] + lags[recv_rows * stations :]
            root_send[side] = lags.astype(jnp.bfloat16)

            @pl.when(sta != 0)
            def _():
                to_root(side, sta).start()

    def all_entered():
        @pl.when(win == 1)
        def _():
            pl.semaphore_wait(barrier, 2 * (last - 1))
            pl.semaphore_signal(ready, inc=1, device_id=(days, sta, 0), device_id_type=MESH)

        @pl.when(win == 0)
        def _():
            pl.semaphore_wait(ready, 1)

    late = sta != 0
    pl.when(late)(all_entered)

    def step_of(n):
        plain = n + jnp.where(n < sta, 0, 1)
        place = n + jnp.where(n < jnp.where(sta == 3, 5, 3 - sta), 0, 1)
        ranked = jnp.int32(0)
        for p, d in enumerate((2, 1, 4, 6, 3, 5, 7)):
            ranked = jnp.where(place == p + 1, d, ranked)
        return across(jnp.where((sta > 0) & (sta < 4), ranked, plain))

    def chunk(n, before):
        pack(step_of(n - 1), *before)
        made = cross(step_of(n))

        @pl.when(late)
        def _():
            push(step_of(n - 1))

        return made

    least = jnp.where(sta == 0, 0, 1)
    before = lax.fori_loop(least + 1, last, chunk, cross(step_of(least)))
    pack(step_of(last - 1), *before)
    mine = cross(0)

    @pl.when(late)
    def _():
        push(step_of(last - 1))

    lags = both(*mine)
    sides = [lags[:, side * half : (side + 1) * half] for side in range(2)]
    own[...] = jnp.where(win == 0, sides[0], sides[1])
    send[0] = jnp.where(win == 0, sides[1], sides[0]).astype(jnp.bfloat16)
    back = pltpu.make_async_remote_copy(
        src_ref=send.at[0],
        dst_ref=recv.at[1],
        send_sem=send_sem,
        recv_sem=recv_sem,
        device_id=(days, sta, 1 - win),
        device_id_type=MESH,
    )
    back.start()

    mask_load.wait()
    source = lax.broadcasted_iota(jnp.int32, (stations, half), 0)
    keep = jnp.zeros((stations, half), jnp.float32)
    for b in range(sta_count):
        keep = jnp.where(source // recv_rows == b, mask_ref[sta, b].astype(jnp.float32), keep)

    def finish(total, rows):
        for r in range(2):
            pair_keep = jnp.where(source == sta * recv_rows + rows[r], 0.0, keep)
            out_ref[rows[r]] = total[r] * pair_keep

    @pl.when(sta == 0)
    def _():
        for which, chips in enumerate((range(1, last - 1), range(last - 1, sta_count))):
            pl.semaphore_wait(came.at[which], len(chips))
            for chip in chips:
                push(chip)

    unit_wait(2 * sta_count - 1, recv_sem)

    @pl.when(sta != 0)
    def _():
        total = [own[...], recv[1].astype(jnp.float32)]
        for step in range(1, sta_count):
            for r in range(2):
                total[r] = total[r] + recv[2 * step + r].astype(jnp.float32)
        finish(total, (win, 1 - win))

    @pl.when(sta == 0)
    def _():
        other = recv[1].astype(jnp.float32)
        total = [jnp.where(win == r, own[...], other) for r in range(2)]
        for m in range(last):
            part = root_recv[m].astype(jnp.float32)
            for r in range(2):
                total[r] = total[r] + part[r * stations : (r + 1) * stations]
        finish(total, (0, 1))

    sent = win_rows + 2 * last - 1

    @pl.when(sta == 0)
    def _():
        unit_wait(sent + 2, send_sem)

    @pl.when((sta != 0) & (win == 0))
    def _():
        unit_wait(sent, send_sem)

    @pl.when((sta != 0) & (win == 1))
    def _():
        unit_wait(sent + 2 * recv_rows, send_sem)


def fused(phases, window_valid, freq_taper, pair_mask):
    sta_count = lax.axis_size("sta")
    win_rows, band, stations = phases.shape
    recv_rows = stations // sta_count
    half = LAGS // 2
    f32, bf16, vmem = jnp.float32, jnp.bfloat16, pltpu.VMEM
    return pl.pallas_call(
        lambda *refs: fused_kernel(*refs, sta_count=sta_count),
        name="fused",
        out_shape=jax.ShapeDtypeStruct((recv_rows, stations, half), f32),
        in_specs=[pl.BlockSpec(memory_space=pltpu.HBM)] * 4,
        out_specs=pl.BlockSpec(memory_space=pltpu.VMEM),
        scratch_shapes=[
            vmem((2, win_rows, stations, band), bf16),
            pltpu.SMEM(window_valid.shape, jnp.int32),
            vmem((freq_taper.shape[0] // 128, 128), f32),
            pltpu.SMEM(pair_mask.shape, jnp.int32),
            vmem((2 * win_rows, stations, band), f32),
            vmem((2 * win_rows, stations, band), f32),
            vmem((band, LAGS), bf16),
            vmem((band, LAGS), bf16),
            vmem((16, LAGS), f32),
            vmem((16, LAGS), f32),
            vmem((1, band), f32),
            vmem((stations, half), f32),
            vmem((2 * sta_count, stations, half), bf16),
            vmem((2 * sta_count, stations, half), bf16),
            vmem((2, recv_rows * stations, half), bf16),
            vmem((sta_count - 1, recv_rows * stations, half), bf16),
            vmem((32, stations, half), bf16),
            pltpu.SemaphoreType.DMA((3,)),
            pltpu.SemaphoreType.DMA((2,)),
            pltpu.SemaphoreType.DMA,
            pltpu.SemaphoreType.DMA,
            pltpu.SemaphoreType.REGULAR,
            pltpu.SemaphoreType.REGULAR((2,)),
        ],
        compiler_params=pltpu.CompilerParams(
            collective_id=0, has_side_effects=True, vmem_limit_bytes=16 * 2**20
        ),
    )(
        *(
            pltpu.with_memory_space_constraint(a, pltpu.HBM)
            for a in (
                jnp.transpose(phases, (0, 2, 1)),
                window_valid,
                freq_taper.reshape(-1, 128),
                pair_mask,
            )
        )
    )


def lag_table(freq_bins, lag_count):
    freq_index = jnp.arange(freq_bins, dtype=jnp.int32)[:, None]
    lag_index = jnp.arange(lag_count, dtype=jnp.int32)[None, :] - lag_count // 2
    wrapped = jnp.mod(freq_index * lag_index, 2 * freq_bins)
    angle = wrapped.astype(jnp.float32) * (math.pi / freq_bins)
    return jnp.stack((jnp.cos(angle), -jnp.sin(angle))).astype(jnp.bfloat16)


def per_device(phases, window_valid, freq_taper, pair_mask):
    sta_count = lax.axis_size("sta")
    win_rows, band_bins, stations = phases.shape
    freq_bins = band_bins * sta_count
    recv_rows = stations // sta_count
    sta_index = lax.axis_index("sta")
    win_group = lax.axis_index("win")
    valid_count = jnp.sum(window_valid.astype(jnp.float32))
    norm_scale = 1.0 / jnp.sqrt(freq_bins * jnp.maximum(valid_count, 1.0))
    bin_weight = freq_taper * norm_scale
    group_valid = lax.dynamic_slice_in_dim(window_valid, win_group * win_rows, win_rows)
    group_weight = group_valid.astype(jnp.bfloat16)[:, None, None]
    own_f = phases.astype(jnp.float32)
    own_cos = jnp.cos(own_f).astype(jnp.bfloat16)
    own_sin = jnp.sin(own_f).astype(jnp.bfloat16)
    left_cos = own_cos * group_weight
    left_sin = own_sin * group_weight
    band_weight = lax.dynamic_slice_in_dim(bin_weight, sta_index * band_bins, band_bins)
    pair_re = jnp.einsum("wki,wkj->ijk", left_cos, own_cos, preferred_element_type=jnp.float32)
    pair_re = pair_re + jnp.einsum(
        "wki,wkj->ijk", left_sin, own_sin, preferred_element_type=jnp.float32
    )
    band_re = (pair_re * band_weight).astype(jnp.bfloat16)
    pair_im = jnp.einsum("wki,wkj->ijk", left_sin, own_cos, preferred_element_type=jnp.float32)
    pair_im = pair_im - jnp.einsum(
        "wki,wkj->ijk", left_cos, own_sin, preferred_element_type=jnp.float32
    )
    band_im = (pair_im * band_weight).astype(jnp.bfloat16)
    spectra = lax.all_to_all(
        jnp.stack((band_re, band_im)), "sta", split_axis=1, concat_axis=3, tiled=True
    )
    lag_count = LAGS
    transform = lag_table(freq_bins, lag_count)
    flat_spectra = spectra.reshape(2, recv_rows * stations, freq_bins)
    correlation = jnp.einsum(
        "cnk,ckt->nt", flat_spectra, transform, preferred_element_type=jnp.float32
    )
    block_row = lax.dynamic_index_in_dim(pair_mask, sta_index, 0, keepdims=False)
    station_row = jnp.repeat(block_row, recv_rows).astype(jnp.float32)
    receiver = sta_index * recv_rows + jnp.arange(recv_rows, dtype=jnp.int32)
    distinct = (receiver[:, None] != jnp.arange(stations, dtype=jnp.int32)[None, :]).astype(
        jnp.float32
    )
    pair_keep = station_row[None, :] * distinct
    correlation = correlation.reshape(recv_rows, stations, lag_count) * pair_keep[:, :, None]
    return lax.psum_scatter(correlation, "win", scatter_dimension=2, tiled=True)


def solution(mesh):
    def body(phases, window_valid, freq_taper, pair_mask):
        win_rows, band, stations = phases.shape
        sta_count, win_count = mesh.shape["sta"], mesh.shape["win"]
        if sta_count == 8 and band == 256 and stations == 16 and win_count == 2 and win_rows == 12:
            return fused(phases, window_valid, freq_taper, pair_mask)
        return per_device(phases, window_valid, freq_taper, pair_mask)

    return jax.shard_map(
        body,
        mesh=mesh,
        in_specs=(P(("days", "win"), "sta", None), P("days"), P(), P()),
        out_specs=P(("days", "sta"), None, "win"),
        check_vma=False,
    )
```

```python
import math

import jax
import jax.numpy as jnp
import numpy as np
from jax import lax
from jax.experimental import pallas as pl
from jax.experimental.pallas import tpu as pltpu
from jax.sharding import PartitionSpec as P

LAGS = 512
MESH = pl.DeviceIdType.MESH


def fit(function, degree):
    nodes = np.polynomial.chebyshev.Chebyshev.interpolate(function, degree, domain=[0.0, math.pi**2])
    return [float(c) for c in nodes.convert(kind=np.polynomial.Polynomial).coef]


ROOT = math.sqrt(2.0)
SIN_COEF = fit(lambda y: ROOT * 0.5 * np.sinc(np.sqrt(y) / (2 * math.pi)), 4)
COS_COEF = fit(lambda y: ROOT * np.cos(0.5 * np.sqrt(y)), 4)


def horner(coef, y):
    total = y * coef[-1] + coef[-2]
    for c in coef[-3::-1]:
        total = total * y + c
    return total


def cos_sin(x, one=1.0):
    y = x * x
    s, c = x * horner(SIN_COEF, y), horner(COS_COEF, y)
    return one - s * s, s * c


def fused_kernel(
    phases_hbm,
    valid_hbm,
    taper_hbm,
    mask_hbm,
    out_ref,
    phases_ref,
    valid_ref,
    taper_ref,
    mask_ref,
    cos_ref,
    sin_ref,
    lag_cos,
    lag_sin,
    turn_cos,
    turn_sin,
    weight_ref,
    own,
    send,
    recv,
    root_send,
    root_recv,
    units,
    keeps,
    load_sem,
    swap_sem,
    send_sem,
    recv_sem,
    ready,
    came,
    *,
    sta_count,
):
    days, sta, win = (lax.axis_index(a) for a in ("days", "sta", "win"))
    win_rows, stations, band = phases_hbm.shape
    recv_rows = stations // sta_count
    freq_bins = band * sta_count
    half = LAGS // 2
    last = sta_count - 1

    parts = swap_sem.shape[0]
    part_rows = win_rows // parts
    cut = win_rows // 3

    def unit_wait(count, sem):
        pltpu.make_async_copy(units.at[:count], units.at[:count], sem).wait()

    def phase_load(n):
        at = pl.ds(n * cut, cut + n * cut)
        return pltpu.make_async_copy(phases_hbm.at[at], phases_ref.at[win, at], load_sem.at[n + 1])

    valid_load = pltpu.make_async_copy(valid_hbm, valid_ref, load_sem.at[0])
    mask_load = pltpu.make_async_copy(mask_hbm, mask_ref, load_sem.at[0])
    taper_load = pltpu.make_async_copy(taper_hbm, taper_ref, load_sem.at[2])
    valid_load.start()
    swaps = [
        pltpu.make_async_remote_copy(
            src_ref=phases_hbm.at[pl.ds(part * part_rows, part_rows)],
            dst_ref=phases_ref.at[win, pl.ds(part * part_rows, part_rows)],
            send_sem=send_sem,
            recv_sem=swap_sem.at[part],
            device_id=(days, sta, 1 - win),
            device_id_type=MESH,
        )
        for part in range(parts)
    ]

    def across(step):
        bits = [2**n for n in range(last.bit_length())]
        return sum(lax.rem(lax.div(sta, n) + lax.div(jnp.int32(step), n), 2) * n for n in bits)

    barrier = pltpu.get_barrier_semaphore()

    @pl.when(win == 1)
    def _():
        pl.semaphore_signal(barrier, inc=1, device_id=(days, sta, 0), device_id_type=MESH)

    @pl.when(sta == 0)
    def _():
        for step in range(last, 0, -1):
            pl.semaphore_signal(barrier, inc=1, device_id=(days, step, 0), device_id_type=MESH)

    @pl.when((win == 0) & (sta == 0))
    def _():
        pl.semaphore_wait(barrier, 1)

    @pl.when((win == 0) & (sta != 0))
    def _():
        pl.semaphore_wait(barrier, 3)

    @pl.when(win == 0)
    def _():
        pl.semaphore_signal(ready, inc=1, device_id=(days, sta, 1), device_id_type=MESH)
        for swap in swaps:
            swap.start()

    for load in (phase_load(0), taper_load, phase_load(1)):
        load.start()

    for chip in range(1, sta_count):

        @pl.when((sta != 0) & (sta != chip))
        def _():
            pl.semaphore_signal(barrier, inc=1, device_id=(days, chip, 1), device_id_type=MESH)

    rows = 16
    lag = lax.broadcasted_iota(jnp.int32, (rows, LAGS), 1) - half
    sub = lax.broadcasted_iota(jnp.int32, (rows, LAGS), 0)

    def turned(k):
        turn = ((k * lag + freq_bins) & (2 * freq_bins - 1)) - freq_bins
        return cos_sin(turn.astype(jnp.float32) * (math.pi / freq_bins))

    fine_cos, fine_sin = turned(sub)
    turn_cos[...], turn_sin[...] = turned(sub * rows + sta * band)

    @pl.when(win == 1)
    def _():
        pl.semaphore_wait(ready, 1)
        for swap in swaps:
            swap.start()

    @pl.when((win == 1) & (sta != 0))
    def _():
        for side in range(2):
            pl.semaphore_signal(
                came.at[lax.div(sta, last - 1)],
                inc=1,
                device_id=(days, 0, side),
                device_id_type=MESH,
            )

    for b in range(band // rows):
        c, s = turn_cos[b : b + 1, :], turn_sin[b : b + 1, :]
        at = slice(b * rows, (b + 1) * rows)
        lag_cos[at, :] = (c * fine_cos - s * fine_sin).astype(jnp.bfloat16)
        lag_sin[at, :] = (-s * fine_cos - c * fine_sin).astype(jnp.bfloat16)

    def phasor(group, w):
        n = group * win_rows + w
        valid = valid_ref[n].astype(jnp.float32)
        c, s = cos_sin(phases_ref[group, w].astype(jnp.float32) * valid, valid)
        c = c.astype(jnp.bfloat16).astype(jnp.float32)
        s = s.astype(jnp.bfloat16).astype(jnp.float32)
        cos_ref[n], sin_ref[n] = c, s
        return c, s

    def cross(step):
        row = across(step) * recv_rows + win
        made = []
        for group in range(2):
            re = jnp.zeros((stations, band), jnp.float32)
            im = jnp.zeros((stations, band), jnp.float32)
            for n in range(group * win_rows, (group + 1) * win_rows):
                cj, sj = cos_ref[n], sin_ref[n]
                ci, si = cos_ref[n, pl.ds(row, 1), :], sin_ref[n, pl.ds(row, 1), :]
                re = re + (ci * cj + si * sj)
                im = im + (si * cj - ci * sj)
            made.append([(x * weight_ref[...]).astype(jnp.bfloat16) for x in (re, im)])
        return [jnp.concatenate(part, axis=0) for part in zip(*made)]

    def to_lags(re, im):
        part = jnp.dot(re, lag_cos[...], preferred_element_type=jnp.float32)
        return part + jnp.dot(im, lag_sin[...], preferred_element_type=jnp.float32)

    def scatter(step, side):
        return pltpu.make_async_remote_copy(
            src_ref=send.at[2 * step + side],
            dst_ref=recv.at[2 * step + lax.rem(win + side, 2)],
            send_sem=send_sem,
            recv_sem=recv_sem,
            device_id=(days, across(step), side),
            device_id_type=MESH,
        )

    def both(re, im):
        lags = to_lags(re, im)
        return lags[:stations] + lags[stations:]

    def pack(step, re, im):
        lags = both(re, im).astype(jnp.bfloat16)
        for side in range(2):
            send[2 * step + side] = lags[:, side * half : (side + 1) * half]

    def push(step):
        for side in range(2):
            scatter(step, side).start()

    def to_root(side, step):
        return pltpu.make_async_remote_copy(
            src_ref=root_send.at[side],
            dst_ref=root_recv.at[step - 1],
            send_sem=send_sem,
            recv_sem=recv_sem,
            device_id=(days, 0, side),
            device_id_type=MESH,
        )

    valid_load.wait()
    mask_load.start()

    def arrive(group):
        if group == 0:
            for n in range(2):
                rows = cut + n * cut
                unit_wait(rows + n, load_sem.at[n + 1])
                yield from range(n * cut, n * cut + rows)
        else:
            for part in range(parts):
                swaps[part].wait_recv()
                yield from range(part * part_rows, (part + 1) * part_rows)

    def norm_weight():
        count = valid_ref[0]
        for w in range(1, valid_ref.shape[0]):
            count = count + valid_ref[w]
        count = jnp.full((1, 128), count, jnp.int32).astype(jnp.float32)
        norm = 1.0 / jnp.sqrt(freq_bins * jnp.maximum(count, 1.0))
        lane_rows = band // 128
        weight_ref[...] = jnp.concatenate(
            [taper_ref[pl.ds(sta * lane_rows + r, 1), :] * norm for r in range(lane_rows)], axis=1
        )

    @pl.when(win == 0)
    def _():
        for group in range(2):
            for w in arrive(group):
                phasor(group, w)
        norm_weight()

    @pl.when(win == 1)
    def _():
        made = []
        for group in range(2):
            re = [jnp.zeros((stations, band), jnp.float32) for _ in range(recv_rows)]
            im = [jnp.zeros((stations, band), jnp.float32) for _ in range(recv_rows)]
            for w in arrive(group):
                cj, sj = phasor(1 - group, w)
                for r in range(recv_rows):
                    ci, si = cj[r : r + 1, :], sj[r : r + 1, :]
                    re[r] = re[r] + (ci * cj + si * sj)
                    im[r] = im[r] + (si * cj - ci * sj)
            if group == 0:
                norm_weight()
            made.append([[(x * weight_ref[...]).astype(jnp.bfloat16) for x in p] for p in (re, im)])
        re, im = [jnp.concatenate(made[0][p] + made[1][p], axis=0) for p in range(2)]
        for side in range(2):
            at = slice(side * half, (side + 1) * half)
            lags = jnp.dot(re, lag_cos[:, at], preferred_element_type=jnp.float32)
            lags = lags + jnp.dot(im, lag_sin[:, at], preferred_element_type=jnp.float32)
            lags = lags[: recv_rows * stations] + lags[recv_rows * stations :]
            root_send[side] = lags.astype(jnp.bfloat16)

            @pl.when(sta != 0)
            def _():
                to_root(side, sta).start()

    def all_entered():
        @pl.when(win == 1)
        def _():
            pl.semaphore_wait(barrier, 2 * (last - 1))
            pl.semaphore_signal(ready, inc=1, device_id=(days, sta, 0), device_id_type=MESH)

        @pl.when(win == 0)
        def _():
            pl.semaphore_wait(ready, 1)

    late = sta != 0
    pl.when(late)(all_entered)

    def step_of(n):
        plain = n + jnp.where(n < sta, 0, 1)
        place = n + jnp.where(n < jnp.where(sta == 3, 5, 3 - sta), 0, 1)
        ranked = jnp.int32(0)
        for p, d in enumerate((2, 1, 4, 6, 3, 5, 7)):
            ranked = jnp.where(place == p + 1, d, ranked)
        return across(jnp.where((sta > 0) & (sta < 4), ranked, plain))

    def chunk(n, before):
        pack(step_of(n - 1), *before)
        made = cross(step_of(n))

        @pl.when(late)
        def _():
            push(step_of(n - 1))

        return made

    least = jnp.where(sta == 0, 0, 1)
    before = lax.fori_loop(least + 1, last, chunk, cross(step_of(least)))
    pack(step_of(last - 1), *before)
    mine = cross(0)

    @pl.when(late)
    def _():
        push(step_of(last - 1))

    lags = both(*mine)
    sides = [lags[:, side * half : (side + 1) * half] for side in range(2)]
    own[...] = jnp.where(win == 0, sides[0], sides[1])
    send[0] = jnp.where(win == 0, sides[1], sides[0]).astype(jnp.bfloat16)
    back = pltpu.make_async_remote_copy(
        src_ref=send.at[0],
        dst_ref=recv.at[1],
        send_sem=send_sem,
        recv_sem=recv_sem,
        device_id=(days, sta, 1 - win),
        device_id_type=MESH,
    )
    back.start()

    mask_load.wait()
    source = lax.broadcasted_iota(jnp.int32, (stations, half), 0)
    keep = jnp.zeros((stations, half), jnp.float32)
    for b in range(sta_count):
        keep = jnp.where(source // recv_rows == b, mask_ref[sta, b].astype(jnp.float32), keep)

    for r in range(recv_rows):
        keeps[r] = jnp.where(source == sta * recv_rows + r, 0.0, keep)

    def finish(total, rows):
        for r in range(2):
            out_ref[rows[r]] = total[r] * keeps[rows[r]]

    @pl.when(sta == 0)
    def _():
        for which, chips in enumerate((range(1, last - 1), range(last - 1, sta_count))):
            pl.semaphore_wait(came.at[which], len(chips))
            for chip in chips:
                push(chip)

    unit_wait(2 * sta_count - 1, recv_sem)

    @pl.when(sta != 0)
    def _():
        total = [own[...], recv[1].astype(jnp.float32)]
        for step in range(1, sta_count):
            for r in range(2):
                total[r] = total[r] + recv[2 * step + r].astype(jnp.float32)
        finish(total, (win, 1 - win))

    @pl.when(sta == 0)
    def _():
        other = recv[1].astype(jnp.float32)
        total = [jnp.where(win == r, own[...], other) for r in range(2)]
        for m in range(last):
            part = root_recv[m].astype(jnp.float32)
            for r in range(2):
                total[r] = total[r] + part[r * stations : (r + 1) * stations]
        finish(total, (0, 1))

    sent = win_rows + 2 * last - 1

    @pl.when(sta == 0)
    def _():
        unit_wait(sent + 2, send_sem)

    @pl.when((sta != 0) & (win == 0))
    def _():
        unit_wait(sent, send_sem)

    @pl.when((sta != 0) & (win == 1))
    def _():
        unit_wait(sent + 2 * recv_rows, send_sem)


def fused(phases, window_valid, freq_taper, pair_mask):
    sta_count = lax.axis_size("sta")
    win_rows, band, stations = phases.shape
    recv_rows = stations // sta_count
    half = LAGS // 2
    f32, bf16, vmem = jnp.float32, jnp.bfloat16, pltpu.VMEM
    return pl.pallas_call(
        lambda *refs: fused_kernel(*refs, sta_count=sta_count),
        name="fused",
        out_shape=jax.ShapeDtypeStruct((recv_rows, stations, half), f32),
        in_specs=[pl.BlockSpec(memory_space=pltpu.HBM)] * 4,
        out_specs=pl.BlockSpec(memory_space=pltpu.VMEM),
        scratch_shapes=[
            vmem((2, win_rows, stations, band), bf16),
            pltpu.SMEM(window_valid.shape, jnp.int32),
            vmem((freq_taper.shape[0] // 128, 128), f32),
            pltpu.SMEM(pair_mask.shape, jnp.int32),
            vmem((2 * win_rows, stations, band), f32),
            vmem((2 * win_rows, stations, band), f32),
            vmem((band, LAGS), bf16),
            vmem((band, LAGS), bf16),
            vmem((16, LAGS), f32),
            vmem((16, LAGS), f32),
            vmem((1, band), f32),
            vmem((stations, half), f32),
            vmem((2 * sta_count, stations, half), bf16),
            vmem((2 * sta_count, stations, half), bf16),
            vmem((2, recv_rows * stations, half), bf16),
            vmem((sta_count - 1, recv_rows * stations, half), bf16),
            vmem((32, stations, half), bf16),
            vmem((recv_rows, stations, half), f32),
            pltpu.SemaphoreType.DMA((3,)),
            pltpu.SemaphoreType.DMA((3,)),
            pltpu.SemaphoreType.DMA,
            pltpu.SemaphoreType.DMA,
            pltpu.SemaphoreType.REGULAR,
            pltpu.SemaphoreType.REGULAR((2,)),
        ],
        compiler_params=pltpu.CompilerParams(
            collective_id=0, has_side_effects=True, vmem_limit_bytes=16 * 2**20
        ),
    )(
        *(
            pltpu.with_memory_space_constraint(a, pltpu.HBM)
            for a in (
                jnp.transpose(phases, (0, 2, 1)),
                window_valid,
                freq_taper.reshape(-1, 128),
                pair_mask,
            )
        )
    )


def lag_table(freq_bins, lag_count):
    freq_index = jnp.arange(freq_bins, dtype=jnp.int32)[:, None]
    lag_index = jnp.arange(lag_count, dtype=jnp.int32)[None, :] - lag_count // 2
    wrapped = jnp.mod(freq_index * lag_index, 2 * freq_bins)
    angle = wrapped.astype(jnp.float32) * (math.pi / freq_bins)
    return jnp.stack((jnp.cos(angle), -jnp.sin(angle))).astype(jnp.bfloat16)


def per_device(phases, window_valid, freq_taper, pair_mask):
    sta_count = lax.axis_size("sta")
    win_rows, band_bins, stations = phases.shape
    freq_bins = band_bins * sta_count
    recv_rows = stations // sta_count
    sta_index = lax.axis_index("sta")
    win_group = lax.axis_index("win")
    valid_count = jnp.sum(window_valid.astype(jnp.float32))
    norm_scale = 1.0 / jnp.sqrt(freq_bins * jnp.maximum(valid_count, 1.0))
    bin_weight = freq_taper * norm_scale
    group_valid = lax.dynamic_slice_in_dim(window_valid, win_group * win_rows, win_rows)
    group_weight = group_valid.astype(jnp.bfloat16)[:, None, None]
    own_f = phases.astype(jnp.float32)
    own_cos = jnp.cos(own_f).astype(jnp.bfloat16)
    own_sin = jnp.sin(own_f).astype(jnp.bfloat16)
    left_cos = own_cos * group_weight
    left_sin = own_sin * group_weight
    band_weight = lax.dynamic_slice_in_dim(bin_weight, sta_index * band_bins, band_bins)
    pair_re = jnp.einsum("wki,wkj->ijk", left_cos, own_cos, preferred_element_type=jnp.float32)
    pair_re = pair_re + jnp.einsum(
        "wki,wkj->ijk", left_sin, own_sin, preferred_element_type=jnp.float32
    )
    band_re = (pair_re * band_weight).astype(jnp.bfloat16)
    pair_im = jnp.einsum("wki,wkj->ijk", left_sin, own_cos, preferred_element_type=jnp.float32)
    pair_im = pair_im - jnp.einsum(
        "wki,wkj->ijk", left_cos, own_sin, preferred_element_type=jnp.float32
    )
    band_im = (pair_im * band_weight).astype(jnp.bfloat16)
    spectra = lax.all_to_all(
        jnp.stack((band_re, band_im)), "sta", split_axis=1, concat_axis=3, tiled=True
    )
    lag_count = LAGS
    transform = lag_table(freq_bins, lag_count)
    flat_spectra = spectra.reshape(2, recv_rows * stations, freq_bins)
    correlation = jnp.einsum(
        "cnk,ckt->nt", flat_spectra, transform, preferred_element_type=jnp.float32
    )
    block_row = lax.dynamic_index_in_dim(pair_mask, sta_index, 0, keepdims=False)
    station_row = jnp.repeat(block_row, recv_rows).astype(jnp.float32)
    receiver = sta_index * recv_rows + jnp.arange(recv_rows, dtype=jnp.int32)
    distinct = (receiver[:, None] != jnp.arange(stations, dtype=jnp.int32)[None, :]).astype(
        jnp.float32
    )
    pair_keep = station_row[None, :] * distinct
    correlation = correlation.reshape(recv_rows, stations, lag_count) * pair_keep[:, :, None]
    return lax.psum_scatter(correlation, "win", scatter_dimension=2, tiled=True)


def solution(mesh):
    def body(phases, window_valid, freq_taper, pair_mask):
        win_rows, band, stations = phases.shape
        sta_count, win_count = mesh.shape["sta"], mesh.shape["win"]
        if sta_count == 8 and band == 256 and stations == 16 and win_count == 2 and win_rows == 12:
            return fused(phases, window_valid, freq_taper, pair_mask)
        return per_device(phases, window_valid, freq_taper, pair_mask)

    return jax.shard_map(
        body,
        mesh=mesh,
        in_specs=(P(("days", "win"), "sta", None), P("days"), P(), P()),
        out_specs=P(("days", "sta"), None, "win"),
        check_vma=False,
    )
```

```python
import math

import jax
import jax.numpy as jnp
import numpy as np
from jax import lax
from jax.experimental import pallas as pl
from jax.experimental.pallas import tpu as pltpu
from jax.sharding import PartitionSpec as P

LAGS = 512
MESH = pl.DeviceIdType.MESH


def fit(function, degree):
    nodes = np.polynomial.chebyshev.Chebyshev.interpolate(function, degree, domain=[0.0, math.pi**2])
    return [float(c) for c in nodes.convert(kind=np.polynomial.Polynomial).coef]


ROOT = math.sqrt(2.0)
SIN_COEF = fit(lambda y: ROOT * 0.5 * np.sinc(np.sqrt(y) / (2 * math.pi)), 4)
COS_COEF = fit(lambda y: ROOT * np.cos(0.5 * np.sqrt(y)), 4)


def horner(coef, y):
    total = y * coef[-1] + coef[-2]
    for c in coef[-3::-1]:
        total = total * y + c
    return total


def cos_sin(x, one=1.0):
    y = x * x
    s, c = x * horner(SIN_COEF, y), horner(COS_COEF, y)
    return one - s * s, s * c


def fused_kernel(
    phases_hbm,
    valid_hbm,
    taper_hbm,
    mask_hbm,
    out_ref,
    phases_ref,
    valid_ref,
    taper_ref,
    mask_ref,
    cos_ref,
    sin_ref,
    lag_cos,
    lag_sin,
    turn_cos,
    turn_sin,
    weight_ref,
    own,
    send,
    recv,
    root_send,
    root_recv,
    units,
    keeps,
    load_sem,
    swap_sem,
    send_sem,
    recv_sem,
    ready,
    came,
    *,
    sta_count,
):
    days, sta, win = (lax.axis_index(a) for a in ("days", "sta", "win"))
    win_rows, stations, band = phases_hbm.shape
    recv_rows = stations // sta_count
    freq_bins = band * sta_count
    half = LAGS // 2
    last = sta_count - 1

    pieces = ((0, win_rows // 3), (win_rows // 3, win_rows))

    def unit_wait(count, sem):
        pltpu.make_async_copy(units.at[:count], units.at[:count], sem).wait()

    def phase_load(n):
        at = pl.ds(pieces[n][0], pieces[n][1] - pieces[n][0])
        return pltpu.make_async_copy(phases_hbm.at[at], phases_ref.at[win, at], load_sem.at[n + 1])

    valid_load = pltpu.make_async_copy(valid_hbm, valid_ref, load_sem.at[0])
    mask_load = pltpu.make_async_copy(mask_hbm, mask_ref, load_sem.at[0])
    taper_load = pltpu.make_async_copy(taper_hbm, taper_ref, load_sem.at[2])
    valid_load.start()
    swaps = [
        pltpu.make_async_remote_copy(
            src_ref=phases_hbm.at[pl.ds(least, most - least)],
            dst_ref=phases_ref.at[win, pl.ds(least, most - least)],
            send_sem=send_sem,
            recv_sem=swap_sem.at[part],
            device_id=(days, sta, 1 - win),
            device_id_type=MESH,
        )
        for part, (least, most) in enumerate(pieces)
    ]

    def across(step):
        bits = [2**n for n in range(last.bit_length())]
        return sum(lax.rem(lax.div(sta, n) + lax.div(jnp.int32(step), n), 2) * n for n in bits)

    barrier = pltpu.get_barrier_semaphore()

    @pl.when(win == 1)
    def _():
        pl.semaphore_signal(barrier, inc=1, device_id=(days, sta, 0), device_id_type=MESH)

    @pl.when(sta == 0)
    def _():
        for step in range(last, 0, -1):
            pl.semaphore_signal(barrier, inc=1, device_id=(days, step, 0), device_id_type=MESH)

    @pl.when((win == 0) & (sta == 0))
    def _():
        pl.semaphore_wait(barrier, 1)

    @pl.when((win == 0) & (sta != 0))
    def _():
        pl.semaphore_wait(barrier, 3)

    @pl.when(win == 0)
    def _():
        pl.semaphore_signal(ready, inc=1, device_id=(days, sta, 1), device_id_type=MESH)
        for swap in swaps:
            swap.start()

    for load in (phase_load(0), taper_load, phase_load(1)):
        load.start()

    for chip in range(1, sta_count):

        @pl.when((sta != 0) & (sta != chip))
        def _():
            pl.semaphore_signal(barrier, inc=1, device_id=(days, chip, 1), device_id_type=MESH)

    rows = 16
    lag = lax.broadcasted_iota(jnp.int32, (rows, LAGS), 1) - half
    sub = lax.broadcasted_iota(jnp.int32, (rows, LAGS), 0)

    def turned(k):
        turn = ((k * lag + freq_bins) & (2 * freq_bins - 1)) - freq_bins
        return cos_sin(turn.astype(jnp.float32) * (math.pi / freq_bins))

    fine_cos, fine_sin = turned(sub)
    turn_cos[...], turn_sin[...] = turned(sub * rows + sta * band)

    @pl.when(win == 1)
    def _():
        pl.semaphore_wait(ready, 1)
        for swap in swaps:
            swap.start()

    @pl.when((win == 1) & (sta != 0))
    def _():
        for side in range(2):
            pl.semaphore_signal(
                came.at[lax.div(sta, last - 1)],
                inc=1,
                device_id=(days, 0, side),
                device_id_type=MESH,
            )

    for b in range(band // rows):
        c, s = turn_cos[b : b + 1, :], turn_sin[b : b + 1, :]
        at = slice(b * rows, (b + 1) * rows)
        lag_cos[at, :] = (c * fine_cos - s * fine_sin).astype(jnp.bfloat16)
        lag_sin[at, :] = (-s * fine_cos - c * fine_sin).astype(jnp.bfloat16)

    def phasor(group, w):
        n = group * win_rows + w
        valid = valid_ref[n].astype(jnp.float32)
        c, s = cos_sin(phases_ref[group, w].astype(jnp.float32) * valid, valid)
        c = c.astype(jnp.bfloat16).astype(jnp.float32)
        s = s.astype(jnp.bfloat16).astype(jnp.float32)
        cos_ref[n], sin_ref[n] = c, s
        return c, s

    def cross(step):
        row = across(step) * recv_rows + win
        made = []
        for group in range(2):
            re = jnp.zeros((stations, band), jnp.float32)
            im = jnp.zeros((stations, band), jnp.float32)
            for n in range(group * win_rows, (group + 1) * win_rows):
                cj, sj = cos_ref[n], sin_ref[n]
                ci, si = cos_ref[n, pl.ds(row, 1), :], sin_ref[n, pl.ds(row, 1), :]
                re = re + (ci * cj + si * sj)
                im = im + (si * cj - ci * sj)
            made.append([(x * weight_ref[...]).astype(jnp.bfloat16) for x in (re, im)])
        return [jnp.concatenate(part, axis=0) for part in zip(*made)]

    def to_lags(re, im):
        part = jnp.dot(re, lag_cos[...], preferred_element_type=jnp.float32)
        return part + jnp.dot(im, lag_sin[...], preferred_element_type=jnp.float32)

    def scatter(step, side):
        return pltpu.make_async_remote_copy(
            src_ref=send.at[2 * step + side],
            dst_ref=recv.at[2 * step + lax.rem(win + side, 2)],
            send_sem=send_sem,
            recv_sem=recv_sem,
            device_id=(days, across(step), side),
            device_id_type=MESH,
        )

    def both(re, im):
        lags = to_lags(re, im)
        return lags[:stations] + lags[stations:]

    def pack(step, re, im):
        lags = both(re, im).astype(jnp.bfloat16)
        for side in range(2):
            send[2 * step + side] = lags[:, side * half : (side + 1) * half]

    def push(step):
        for side in range(2):
            scatter(step, side).start()

    def to_root(side, step):
        return pltpu.make_async_remote_copy(
            src_ref=root_send.at[side],
            dst_ref=root_recv.at[step - 1],
            send_sem=send_sem,
            recv_sem=recv_sem,
            device_id=(days, 0, side),
            device_id_type=MESH,
        )

    valid_load.wait()
    mask_load.start()

    def arrive(group):
        for n, (least, most) in enumerate(pieces):
            if group == 0:
                unit_wait(most - least + n, load_sem.at[n + 1])
            else:
                swaps[n].wait_recv()
            yield from range(least, most)

    def norm_weight():
        count = valid_ref[0]
        for w in range(1, valid_ref.shape[0]):
            count = count + valid_ref[w]
        count = jnp.full((1, 128), count, jnp.int32).astype(jnp.float32)
        norm = 1.0 / jnp.sqrt(freq_bins * jnp.maximum(count, 1.0))
        lane_rows = band // 128
        weight_ref[...] = jnp.concatenate(
            [taper_ref[pl.ds(sta * lane_rows + r, 1), :] * norm for r in range(lane_rows)], axis=1
        )

    @pl.when(win == 0)
    def _():
        for group in range(2):
            for w in arrive(group):
                phasor(group, w)
        norm_weight()

    @pl.when(win == 1)
    def _():
        made = []
        for group in range(2):
            re = [jnp.zeros((stations, band), jnp.float32) for _ in range(recv_rows)]
            im = [jnp.zeros((stations, band), jnp.float32) for _ in range(recv_rows)]
            for w in arrive(group):
                cj, sj = phasor(1 - group, w)
                for r in range(recv_rows):
                    ci, si = cj[r : r + 1, :], sj[r : r + 1, :]
                    re[r] = re[r] + (ci * cj + si * sj)
                    im[r] = im[r] + (si * cj - ci * sj)
            if group == 0:
                norm_weight()
            made.append([[(x * weight_ref[...]).astype(jnp.bfloat16) for x in p] for p in (re, im)])
        re, im = [jnp.concatenate(made[0][p] + made[1][p], axis=0) for p in range(2)]
        for side in range(2):
            at = slice(side * half, (side + 1) * half)
            lags = jnp.dot(re, lag_cos[:, at], preferred_element_type=jnp.float32)
            lags = lags + jnp.dot(im, lag_sin[:, at], preferred_element_type=jnp.float32)
            lags = lags[: recv_rows * stations] + lags[recv_rows * stations :]
            root_send[side] = lags.astype(jnp.bfloat16)

            @pl.when(sta != 0)
            def _():
                to_root(side, sta).start()

    def all_entered():
        @pl.when(win == 1)
        def _():
            pl.semaphore_wait(barrier, 2 * (last - 1))
            pl.semaphore_signal(ready, inc=1, device_id=(days, sta, 0), device_id_type=MESH)

        @pl.when(win == 0)
        def _():
            pl.semaphore_wait(ready, 1)

    late = sta != 0
    pl.when(late)(all_entered)

    def step_of(n):
        plain = n + jnp.where(n < sta, 0, 1)
        place = n + jnp.where(n < jnp.where(sta == 3, 5, 3 - sta), 0, 1)
        ranked = jnp.int32(0)
        for p, d in enumerate((2, 1, 4, 6, 3, 5, 7)):
            ranked = jnp.where(place == p + 1, d, ranked)
        return across(jnp.where((sta > 0) & (sta < 4), ranked, plain))

    def chunk(n, before):
        pack(step_of(n - 1), *before)
        made = cross(step_of(n))

        @pl.when(late)
        def _():
            push(step_of(n - 1))

        return made

    least = jnp.where(sta == 0, 0, 1)
    before = lax.fori_loop(least + 1, last, chunk, cross(step_of(least)))
    pack(step_of(last - 1), *before)
    mine = cross(0)

    @pl.when(late)
    def _():
        push(step_of(last - 1))

    lags = both(*mine)
    sides = [lags[:, side * half : (side + 1) * half] for side in range(2)]
    own[...] = jnp.where(win == 0, sides[0], sides[1])
    send[0] = jnp.where(win == 0, sides[1], sides[0]).astype(jnp.bfloat16)
    back = pltpu.make_async_remote_copy(
        src_ref=send.at[0],
        dst_ref=recv.at[1],
        send_sem=send_sem,
        recv_sem=recv_sem,
        device_id=(days, sta, 1 - win),
        device_id_type=MESH,
    )
    back.start()

    mask_load.wait()
    source = lax.broadcasted_iota(jnp.int32, (stations, half), 0)
    keep = jnp.zeros((stations, half), jnp.float32)
    for b in range(sta_count):
        keep = jnp.where(source // recv_rows == b, mask_ref[sta, b].astype(jnp.float32), keep)

    for r in range(recv_rows):
        keeps[r] = jnp.where(source == sta * recv_rows + r, 0.0, keep)

    def finish(total, rows):
        for r in range(2):
            out_ref[rows[r]] = total[r] * keeps[rows[r]]

    @pl.when(sta == 0)
    def _():
        for which, chips in enumerate((range(1, last - 1), range(last - 1, sta_count))):
            pl.semaphore_wait(came.at[which], len(chips))
            for chip in chips:
                push(chip)

    unit_wait(2 * sta_count - 1, recv_sem)

    @pl.when(sta != 0)
    def _():
        total = [own[...], recv[1].astype(jnp.float32)]
        for step in range(1, sta_count):
            for r in range(2):
                total[r] = total[r] + recv[2 * step + r].astype(jnp.float32)
        finish(total, (win, 1 - win))

    @pl.when(sta == 0)
    def _():
        other = recv[1].astype(jnp.float32)
        total = [jnp.where(win == r, own[...], other) for r in range(2)]
        for m in range(last):
            part = root_recv[m].astype(jnp.float32)
            for r in range(2):
                total[r] = total[r] + part[r * stations : (r + 1) * stations]
        finish(total, (0, 1))

    sent = win_rows + 2 * last - 1

    @pl.when(sta == 0)
    def _():
        unit_wait(sent + 2, send_sem)

    @pl.when((sta != 0) & (win == 0))
    def _():
        unit_wait(sent, send_sem)

    @pl.when((sta != 0) & (win == 1))
    def _():
        unit_wait(sent + 2 * recv_rows, send_sem)


def fused(phases, window_valid, freq_taper, pair_mask):
    sta_count = lax.axis_size("sta")
    win_rows, band, stations = phases.shape
    recv_rows = stations // sta_count
    half = LAGS // 2
    f32, bf16, vmem = jnp.float32, jnp.bfloat16, pltpu.VMEM
    return pl.pallas_call(
        lambda *refs: fused_kernel(*refs, sta_count=sta_count),
        name="fused",
        out_shape=jax.ShapeDtypeStruct((recv_rows, stations, half), f32),
        in_specs=[pl.BlockSpec(memory_space=pltpu.HBM)] * 4,
        out_specs=pl.BlockSpec(memory_space=pltpu.VMEM),
        scratch_shapes=[
            vmem((2, win_rows, stations, band), bf16),
            pltpu.SMEM(window_valid.shape, jnp.int32),
            vmem((freq_taper.shape[0] // 128, 128), f32),
            pltpu.SMEM(pair_mask.shape, jnp.int32),
            vmem((2 * win_rows, stations, band), f32),
            vmem((2 * win_rows, stations, band), f32),
            vmem((band, LAGS), bf16),
            vmem((band, LAGS), bf16),
            vmem((16, LAGS), f32),
            vmem((16, LAGS), f32),
            vmem((1, band), f32),
            vmem((stations, half), f32),
            vmem((2 * sta_count, stations, half), bf16),
            vmem((2 * sta_count, stations, half), bf16),
            vmem((2, recv_rows * stations, half), bf16),
            vmem((sta_count - 1, recv_rows * stations, half), bf16),
            vmem((32, stations, half), bf16),
            vmem((recv_rows, stations, half), f32),
            pltpu.SemaphoreType.DMA((3,)),
            pltpu.SemaphoreType.DMA((2,)),
            pltpu.SemaphoreType.DMA,
            pltpu.SemaphoreType.DMA,
            pltpu.SemaphoreType.REGULAR,
            pltpu.SemaphoreType.REGULAR((2,)),
        ],
        compiler_params=pltpu.CompilerParams(
            collective_id=0, has_side_effects=True, vmem_limit_bytes=16 * 2**20
        ),
    )(
        *(
            pltpu.with_memory_space_constraint(a, pltpu.HBM)
            for a in (
                jnp.transpose(phases, (0, 2, 1)),
                window_valid,
                freq_taper.reshape(-1, 128),
                pair_mask,
            )
        )
    )


def lag_table(freq_bins, lag_count):
    freq_index = jnp.arange(freq_bins, dtype=jnp.int32)[:, None]
    lag_index = jnp.arange(lag_count, dtype=jnp.int32)[None, :] - lag_count // 2
    wrapped = jnp.mod(freq_index * lag_index, 2 * freq_bins)
    angle = wrapped.astype(jnp.float32) * (math.pi / freq_bins)
    return jnp.stack((jnp.cos(angle), -jnp.sin(angle))).astype(jnp.bfloat16)


def per_device(phases, window_valid, freq_taper, pair_mask):
    sta_count = lax.axis_size("sta")
    win_rows, band_bins, stations = phases.shape
    freq_bins = band_bins * sta_count
    recv_rows = stations // sta_count
    sta_index = lax.axis_index("sta")
    win_group = lax.axis_index("win")
    valid_count = jnp.sum(window_valid.astype(jnp.float32))
    norm_scale = 1.0 / jnp.sqrt(freq_bins * jnp.maximum(valid_count, 1.0))
    bin_weight = freq_taper * norm_scale
    group_valid = lax.dynamic_slice_in_dim(window_valid, win_group * win_rows, win_rows)
    group_weight = group_valid.astype(jnp.bfloat16)[:, None, None]
    own_f = phases.astype(jnp.float32)
    own_cos = jnp.cos(own_f).astype(jnp.bfloat16)
    own_sin = jnp.sin(own_f).astype(jnp.bfloat16)
    left_cos = own_cos * group_weight
    left_sin = own_sin * group_weight
    band_weight = lax.dynamic_slice_in_dim(bin_weight, sta_index * band_bins, band_bins)
    pair_re = jnp.einsum("wki,wkj->ijk", left_cos, own_cos, preferred_element_type=jnp.float32)
    pair_re = pair_re + jnp.einsum(
        "wki,wkj->ijk", left_sin, own_sin, preferred_element_type=jnp.float32
    )
    band_re = (pair_re * band_weight).astype(jnp.bfloat16)
    pair_im = jnp.einsum("wki,wkj->ijk", left_sin, own_cos, preferred_element_type=jnp.float32)
    pair_im = pair_im - jnp.einsum(
        "wki,wkj->ijk", left_cos, own_sin, preferred_element_type=jnp.float32
    )
    band_im = (pair_im * band_weight).astype(jnp.bfloat16)
    spectra = lax.all_to_all(
        jnp.stack((band_re, band_im)), "sta", split_axis=1, concat_axis=3, tiled=True
    )
    lag_count = LAGS
    transform = lag_table(freq_bins, lag_count)
    flat_spectra = spectra.reshape(2, recv_rows * stations, freq_bins)
    correlation = jnp.einsum(
        "cnk,ckt->nt", flat_spectra, transform, preferred_element_type=jnp.float32
    )
    block_row = lax.dynamic_index_in_dim(pair_mask, sta_index, 0, keepdims=False)
    station_row = jnp.repeat(block_row, recv_rows).astype(jnp.float32)
    receiver = sta_index * recv_rows + jnp.arange(recv_rows, dtype=jnp.int32)
    distinct = (receiver[:, None] != jnp.arange(stations, dtype=jnp.int32)[None, :]).astype(
        jnp.float32
    )
    pair_keep = station_row[None, :] * distinct
    correlation = correlation.reshape(recv_rows, stations, lag_count) * pair_keep[:, :, None]
    return lax.psum_scatter(correlation, "win", scatter_dimension=2, tiled=True)


def solution(mesh):
    def body(phases, window_valid, freq_taper, pair_mask):
        win_rows, band, stations = phases.shape
        sta_count, win_count = mesh.shape["sta"], mesh.shape["win"]
        if sta_count == 8 and band == 256 and stations == 16 and win_count == 2 and win_rows == 12:
            return fused(phases, window_valid, freq_taper, pair_mask)
        return per_device(phases, window_valid, freq_taper, pair_mask)

    return jax.shard_map(
        body,
        mesh=mesh,
        in_specs=(P(("days", "win"), "sta", None), P("days"), P(), P()),
        out_specs=P(("days", "sta"), None, "win"),
        check_vma=False,
    )
```

```python
import math

import jax
import jax.numpy as jnp
import numpy as np
from jax import lax
from jax.experimental import pallas as pl
from jax.experimental.pallas import tpu as pltpu
from jax.sharding import PartitionSpec as P

LAGS = 512
MESH = pl.DeviceIdType.MESH


def fit(function, degree):
    nodes = np.polynomial.chebyshev.Chebyshev.interpolate(function, degree, domain=[0.0, math.pi**2])
    return [float(c) for c in nodes.convert(kind=np.polynomial.Polynomial).coef]


ROOT = math.sqrt(2.0)
SIN_COEF = fit(lambda y: ROOT * 0.5 * np.sinc(np.sqrt(y) / (2 * math.pi)), 4)
COS_COEF = fit(lambda y: ROOT * np.cos(0.5 * np.sqrt(y)), 4)


def horner(coef, y):
    total = y * coef[-1] + coef[-2]
    for c in coef[-3::-1]:
        total = total * y + c
    return total


def cos_sin(x, one=1.0):
    y = x * x
    s, c = x * horner(SIN_COEF, y), horner(COS_COEF, y)
    return one - s * s, s * c


def fused_kernel(
    phases_hbm,
    valid_hbm,
    taper_hbm,
    mask_hbm,
    out_ref,
    phases_ref,
    valid_ref,
    taper_ref,
    mask_ref,
    cos_ref,
    sin_ref,
    lag_cos,
    lag_sin,
    turn_cos,
    turn_sin,
    weight_ref,
    own,
    send,
    recv,
    root_send,
    root_recv,
    units,
    keeps,
    load_sem,
    swap_sem,
    send_sem,
    recv_sem,
    ready,
    came,
    *,
    sta_count,
):
    days, sta, win = (lax.axis_index(a) for a in ("days", "sta", "win"))
    win_rows, stations, band = phases_hbm.shape
    recv_rows = stations // sta_count
    freq_bins = band * sta_count
    half = LAGS // 2
    last = sta_count - 1

    pieces = ((0, win_rows // 2), (win_rows // 2, win_rows))

    def unit_wait(count, sem):
        pltpu.make_async_copy(units.at[:count], units.at[:count], sem).wait()

    def phase_load(n):
        at = pl.ds(pieces[n][0], pieces[n][1] - pieces[n][0])
        return pltpu.make_async_copy(phases_hbm.at[at], phases_ref.at[win, at], load_sem.at[n + 1])

    valid_load = pltpu.make_async_copy(valid_hbm, valid_ref, load_sem.at[0])
    mask_load = pltpu.make_async_copy(mask_hbm, mask_ref, load_sem.at[0])
    taper_load = pltpu.make_async_copy(taper_hbm, taper_ref, load_sem.at[2])
    valid_load.start()
    swaps = [
        pltpu.make_async_remote_copy(
            src_ref=phases_hbm.at[pl.ds(least, most - least)],
            dst_ref=phases_ref.at[win, pl.ds(least, most - least)],
            send_sem=send_sem,
            recv_sem=swap_sem.at[part],
            device_id=(days, sta, 1 - win),
            device_id_type=MESH,
        )
        for part, (least, most) in enumerate(pieces)
    ]

    def across(step):
        bits = [2**n for n in range(last.bit_length())]
        return sum(lax.rem(lax.div(sta, n) + lax.div(jnp.int32(step), n), 2) * n for n in bits)

    barrier = pltpu.get_barrier_semaphore()

    @pl.when(win == 1)
    def _():
        pl.semaphore_signal(barrier, inc=1, device_id=(days, sta, 0), device_id_type=MESH)

    @pl.when(sta == 0)
    def _():
        for step in range(last, 0, -1):
            pl.semaphore_signal(barrier, inc=1, device_id=(days, step, 0), device_id_type=MESH)

    @pl.when((win == 0) & (sta == 0))
    def _():
        pl.semaphore_wait(barrier, 1)

    @pl.when((win == 0) & (sta != 0))
    def _():
        pl.semaphore_wait(barrier, 3)

    @pl.when(win == 0)
    def _():
        pl.semaphore_signal(ready, inc=1, device_id=(days, sta, 1), device_id_type=MESH)
        for swap in swaps:
            swap.start()

    for load in (phase_load(0), taper_load, phase_load(1)):
        load.start()

    for chip in range(1, sta_count):

        @pl.when((sta != 0) & (sta != chip))
        def _():
            pl.semaphore_signal(barrier, inc=1, device_id=(days, chip, 1), device_id_type=MESH)

    rows = 16
    lag = lax.broadcasted_iota(jnp.int32, (rows, LAGS), 1) - half
    sub = lax.broadcasted_iota(jnp.int32, (rows, LAGS), 0)

    def turned(k):
        turn = ((k * lag + freq_bins) & (2 * freq_bins - 1)) - freq_bins
        return cos_sin(turn.astype(jnp.float32) * (math.pi / freq_bins))

    fine_cos, fine_sin = turned(sub)
    turn_cos[...], turn_sin[...] = turned(sub * rows + sta * band)

    @pl.when(win == 1)
    def _():
        pl.semaphore_wait(ready, 1)
        for swap in swaps:
            swap.start()

    @pl.when((win == 1) & (sta != 0))
    def _():
        for side in range(2):
            pl.semaphore_signal(
                came.at[lax.div(sta, last - 1)],
                inc=1,
                device_id=(days, 0, side),
                device_id_type=MESH,
            )

    for b in range(band // rows):
        c, s = turn_cos[b : b + 1, :], turn_sin[b : b + 1, :]
        at = slice(b * rows, (b + 1) * rows)
        lag_cos[at, :] = (c * fine_cos - s * fine_sin).astype(jnp.bfloat16)
        lag_sin[at, :] = (-s * fine_cos - c * fine_sin).astype(jnp.bfloat16)

    def phasor(group, w):
        n = group * win_rows + w
        valid = valid_ref[n].astype(jnp.float32)
        c, s = cos_sin(phases_ref[group, w].astype(jnp.float32) * valid, valid)
        c = c.astype(jnp.bfloat16).astype(jnp.float32)
        s = s.astype(jnp.bfloat16).astype(jnp.float32)
        cos_ref[n], sin_ref[n] = c, s
        return c, s

    def cross(step):
        row = across(step) * recv_rows + win
        made = []
        for group in range(2):
            re = jnp.zeros((stations, band), jnp.float32)
            im = jnp.zeros((stations, band), jnp.float32)
            for n in range(group * win_rows, (group + 1) * win_rows):
                cj, sj = cos_ref[n], sin_ref[n]
                ci, si = cos_ref[n, pl.ds(row, 1), :], sin_ref[n, pl.ds(row, 1), :]
                re = re + (ci * cj + si * sj)
                im = im + (si * cj - ci * sj)
            made.append([(x * weight_ref[...]).astype(jnp.bfloat16) for x in (re, im)])
        return [jnp.concatenate(part, axis=0) for part in zip(*made)]

    def to_lags(re, im):
        part = jnp.dot(re, lag_cos[...], preferred_element_type=jnp.float32)
        return part + jnp.dot(im, lag_sin[...], preferred_element_type=jnp.float32)

    def scatter(step, side):
        return pltpu.make_async_remote_copy(
            src_ref=send.at[2 * step + side],
            dst_ref=recv.at[2 * step + lax.rem(win + side, 2)],
            send_sem=send_sem,
            recv_sem=recv_sem,
            device_id=(days, across(step), side),
            device_id_type=MESH,
        )

    def both(re, im):
        lags = to_lags(re, im)
        return lags[:stations] + lags[stations:]

    def pack(step, re, im):
        lags = both(re, im).astype(jnp.bfloat16)
        for side in range(2):
            send[2 * step + side] = lags[:, side * half : (side + 1) * half]

    def push(step):
        for side in range(2):
            scatter(step, side).start()

    def to_root(side, step):
        return pltpu.make_async_remote_copy(
            src_ref=root_send.at[side],
            dst_ref=root_recv.at[step - 1],
            send_sem=send_sem,
            recv_sem=recv_sem,
            device_id=(days, 0, side),
            device_id_type=MESH,
        )

    valid_load.wait()
    mask_load.start()

    def arrive(group):
        for n, (least, most) in enumerate(pieces):
            if group == 0:
                unit_wait(most - least + n, load_sem.at[n + 1])
            else:
                swaps[n].wait_recv()
            yield from range(least, most)

    def norm_weight():
        count = valid_ref[0]
        for w in range(1, valid_ref.shape[0]):
            count = count + valid_ref[w]
        count = jnp.full((1, 128), count, jnp.int32).astype(jnp.float32)
        norm = 1.0 / jnp.sqrt(freq_bins * jnp.maximum(count, 1.0))
        lane_rows = band // 128
        weight_ref[...] = jnp.concatenate(
            [taper_ref[pl.ds(sta * lane_rows + r, 1), :] * norm for r in range(lane_rows)], axis=1
        )

    @pl.when(win == 0)
    def _():
        for group in range(2):
            for w in arrive(group):
                phasor(group, w)
        norm_weight()

    @pl.when(win == 1)
    def _():
        made = []
        for group in range(2):
            re = [jnp.zeros((stations, band), jnp.float32) for _ in range(recv_rows)]
            im = [jnp.zeros((stations, band), jnp.float32) for _ in range(recv_rows)]
            for w in arrive(group):
                cj, sj = phasor(1 - group, w)
                for r in range(recv_rows):
                    ci, si = cj[r : r + 1, :], sj[r : r + 1, :]
                    re[r] = re[r] + (ci * cj + si * sj)
                    im[r] = im[r] + (si * cj - ci * sj)
            if group == 0:
                norm_weight()
            made.append([[(x * weight_ref[...]).astype(jnp.bfloat16) for x in p] for p in (re, im)])
        re, im = [jnp.concatenate(made[0][p] + made[1][p], axis=0) for p in range(2)]
        for side in range(2):
            at = slice(side * half, (side + 1) * half)
            lags = jnp.dot(re, lag_cos[:, at], preferred_element_type=jnp.float32)
            lags = lags + jnp.dot(im, lag_sin[:, at], preferred_element_type=jnp.float32)
            lags = lags[: recv_rows * stations] + lags[recv_rows * stations :]
            root_send[side] = lags.astype(jnp.bfloat16)

            @pl.when(sta != 0)
            def _():
                to_root(side, sta).start()

    def all_entered():
        @pl.when(win == 1)
        def _():
            pl.semaphore_wait(barrier, 2 * (last - 1))
            pl.semaphore_signal(ready, inc=1, device_id=(days, sta, 0), device_id_type=MESH)

        @pl.when(win == 0)
        def _():
            pl.semaphore_wait(ready, 1)

    late = sta != 0
    pl.when(late)(all_entered)

    def step_of(n):
        plain = n + jnp.where(n < sta, 0, 1)
        place = n + jnp.where(n < jnp.where(sta == 3, 5, 3 - sta), 0, 1)
        ranked = jnp.int32(0)
        for p, d in enumerate((2, 1, 4, 6, 3, 5, 7)):
            ranked = jnp.where(place == p + 1, d, ranked)
        return across(jnp.where((sta > 0) & (sta < 4), ranked, plain))

    def chunk(n, before):
        pack(step_of(n - 1), *before)
        made = cross(step_of(n))

        @pl.when(late)
        def _():
            push(step_of(n - 1))

        return made

    least = jnp.where(sta == 0, 0, 1)
    before = lax.fori_loop(least + 1, last, chunk, cross(step_of(least)))
    pack(step_of(last - 1), *before)
    mine = cross(0)

    @pl.when(late)
    def _():
        push(step_of(last - 1))

    lags = both(*mine)
    sides = [lags[:, side * half : (side + 1) * half] for side in range(2)]
    own[...] = jnp.where(win == 0, sides[0], sides[1])
    send[0] = jnp.where(win == 0, sides[1], sides[0]).astype(jnp.bfloat16)
    back = pltpu.make_async_remote_copy(
        src_ref=send.at[0],
        dst_ref=recv.at[1],
        send_sem=send_sem,
        recv_sem=recv_sem,
        device_id=(days, sta, 1 - win),
        device_id_type=MESH,
    )
    back.start()

    mask_load.wait()
    source = lax.broadcasted_iota(jnp.int32, (stations, half), 0)
    keep = jnp.zeros((stations, half), jnp.float32)
    for b in range(sta_count):
        keep = jnp.where(source // recv_rows == b, mask_ref[sta, b].astype(jnp.float32), keep)

    for r in range(recv_rows):
        keeps[r] = jnp.where(source == sta * recv_rows + r, 0.0, keep)

    def finish(total, rows):
        for r in range(2):
            out_ref[rows[r]] = total[r] * keeps[rows[r]]

    @pl.when(sta == 0)
    def _():
        for which, chips in enumerate((range(1, last - 1), range(last - 1, sta_count))):
            pl.semaphore_wait(came.at[which], len(chips))
            for chip in chips:
                push(chip)

    unit_wait(2 * sta_count - 1, recv_sem)

    @pl.when(sta != 0)
    def _():
        total = [own[...], recv[1].astype(jnp.float32)]
        for step in range(1, sta_count):
            for r in range(2):
                total[r] = total[r] + recv[2 * step + r].astype(jnp.float32)
        finish(total, (win, 1 - win))

    @pl.when(sta == 0)
    def _():
        other = recv[1].astype(jnp.float32)
        total = [jnp.where(win == r, own[...], other) for r in range(2)]
        for m in range(last):
            part = root_recv[m].astype(jnp.float32)
            for r in range(2):
                total[r] = total[r] + part[r * stations : (r + 1) * stations]
        finish(total, (0, 1))

    sent = win_rows + 2 * last - 1

    @pl.when(sta == 0)
    def _():
        unit_wait(sent + 2, send_sem)

    @pl.when((sta != 0) & (win == 0))
    def _():
        unit_wait(sent, send_sem)

    @pl.when((sta != 0) & (win == 1))
    def _():
        unit_wait(sent + 2 * recv_rows, send_sem)


def fused(phases, window_valid, freq_taper, pair_mask):
    sta_count = lax.axis_size("sta")
    win_rows, band, stations = phases.shape
    recv_rows = stations // sta_count
    half = LAGS // 2
    f32, bf16, vmem = jnp.float32, jnp.bfloat16, pltpu.VMEM
    return pl.pallas_call(
        lambda *refs: fused_kernel(*refs, sta_count=sta_count),
        name="fused",
        out_shape=jax.ShapeDtypeStruct((recv_rows, stations, half), f32),
        in_specs=[pl.BlockSpec(memory_space=pltpu.HBM)] * 4,
        out_specs=pl.BlockSpec(memory_space=pltpu.VMEM),
        scratch_shapes=[
            vmem((2, win_rows, stations, band), bf16),
            pltpu.SMEM(window_valid.shape, jnp.int32),
            vmem((freq_taper.shape[0] // 128, 128), f32),
            pltpu.SMEM(pair_mask.shape, jnp.int32),
            vmem((2 * win_rows, stations, band), f32),
            vmem((2 * win_rows, stations, band), f32),
            vmem((band, LAGS), bf16),
            vmem((band, LAGS), bf16),
            vmem((16, LAGS), f32),
            vmem((16, LAGS), f32),
            vmem((1, band), f32),
            vmem((stations, half), f32),
            vmem((2 * sta_count, stations, half), bf16),
            vmem((2 * sta_count, stations, half), bf16),
            vmem((2, recv_rows * stations, half), bf16),
            vmem((sta_count - 1, recv_rows * stations, half), bf16),
            vmem((32, stations, half), bf16),
            vmem((recv_rows, stations, half), f32),
            pltpu.SemaphoreType.DMA((3,)),
            pltpu.SemaphoreType.DMA((2,)),
            pltpu.SemaphoreType.DMA,
            pltpu.SemaphoreType.DMA,
            pltpu.SemaphoreType.REGULAR,
            pltpu.SemaphoreType.REGULAR((2,)),
        ],
        compiler_params=pltpu.CompilerParams(
            collective_id=0, has_side_effects=True, vmem_limit_bytes=16 * 2**20
        ),
    )(
        *(
            pltpu.with_memory_space_constraint(a, pltpu.HBM)
            for a in (
                jnp.transpose(phases, (0, 2, 1)),
                window_valid,
                freq_taper.reshape(-1, 128),
                pair_mask,
            )
        )
    )


def lag_table(freq_bins, lag_count):
    freq_index = jnp.arange(freq_bins, dtype=jnp.int32)[:, None]
    lag_index = jnp.arange(lag_count, dtype=jnp.int32)[None, :] - lag_count // 2
    wrapped = jnp.mod(freq_index * lag_index, 2 * freq_bins)
    angle = wrapped.astype(jnp.float32) * (math.pi / freq_bins)
    return jnp.stack((jnp.cos(angle), -jnp.sin(angle))).astype(jnp.bfloat16)


def per_device(phases, window_valid, freq_taper, pair_mask):
    sta_count = lax.axis_size("sta")
    win_rows, band_bins, stations = phases.shape
    freq_bins = band_bins * sta_count
    recv_rows = stations // sta_count
    sta_index = lax.axis_index("sta")
    win_group = lax.axis_index("win")
    valid_count = jnp.sum(window_valid.astype(jnp.float32))
    norm_scale = 1.0 / jnp.sqrt(freq_bins * jnp.maximum(valid_count, 1.0))
    bin_weight = freq_taper * norm_scale
    group_valid = lax.dynamic_slice_in_dim(window_valid, win_group * win_rows, win_rows)
    group_weight = group_valid.astype(jnp.bfloat16)[:, None, None]
    own_f = phases.astype(jnp.float32)
    own_cos = jnp.cos(own_f).astype(jnp.bfloat16)
    own_sin = jnp.sin(own_f).astype(jnp.bfloat16)
    left_cos = own_cos * group_weight
    left_sin = own_sin * group_weight
    band_weight = lax.dynamic_slice_in_dim(bin_weight, sta_index * band_bins, band_bins)
    pair_re = jnp.einsum("wki,wkj->ijk", left_cos, own_cos, preferred_element_type=jnp.float32)
    pair_re = pair_re + jnp.einsum(
        "wki,wkj->ijk", left_sin, own_sin, preferred_element_type=jnp.float32
    )
    band_re = (pair_re * band_weight).astype(jnp.bfloat16)
    pair_im = jnp.einsum("wki,wkj->ijk", left_sin, own_cos, preferred_element_type=jnp.float32)
    pair_im = pair_im - jnp.einsum(
        "wki,wkj->ijk", left_cos, own_sin, preferred_element_type=jnp.float32
    )
    band_im = (pair_im * band_weight).astype(jnp.bfloat16)
    spectra = lax.all_to_all(
        jnp.stack((band_re, band_im)), "sta", split_axis=1, concat_axis=3, tiled=True
    )
    lag_count = LAGS
    transform = lag_table(freq_bins, lag_count)
    flat_spectra = spectra.reshape(2, recv_rows * stations, freq_bins)
    correlation = jnp.einsum(
        "cnk,ckt->nt", flat_spectra, transform, preferred_element_type=jnp.float32
    )
    block_row = lax.dynamic_index_in_dim(pair_mask, sta_index, 0, keepdims=False)
    station_row = jnp.repeat(block_row, recv_rows).astype(jnp.float32)
    receiver = sta_index * recv_rows + jnp.arange(recv_rows, dtype=jnp.int32)
    distinct = (receiver[:, None] != jnp.arange(stations, dtype=jnp.int32)[None, :]).astype(
        jnp.float32
    )
    pair_keep = station_row[None, :] * distinct
    correlation = correlation.reshape(recv_rows, stations, lag_count) * pair_keep[:, :, None]
    return lax.psum_scatter(correlation, "win", scatter_dimension=2, tiled=True)


def solution(mesh):
    def body(phases, window_valid, freq_taper, pair_mask):
        win_rows, band, stations = phases.shape
        sta_count, win_count = mesh.shape["sta"], mesh.shape["win"]
        if sta_count == 8 and band == 256 and stations == 16 and win_count == 2 and win_rows == 12:
            return fused(phases, window_valid, freq_taper, pair_mask)
        return per_device(phases, window_valid, freq_taper, pair_mask)

    return jax.shard_map(
        body,
        mesh=mesh,
        in_specs=(P(("days", "win"), "sta", None), P("days"), P(), P()),
        out_specs=P(("days", "sta"), None, "win"),
        check_vma=False,
    )
```
